32 devices in a mesh: section: 2 (over core), group: 4 (over y, x), dp: 4 (over z).
Axes of the slice: x: 2, y: 2, z: 4, core: 2. Of those that a mesh axis runs over, the one named last changes fastest.
Arguments:
- tokens: bfloat16 [2, 4096, 768], P(None, ('group', 'dp')), may hold values from -6 to 6
- cotangent: bfloat16 [2, 4096, 768], P(None, ('group', 'dp')), may hold values from -6 to 6
- lengths: int32 [2, 16, 3], P(None, ('group', 'dp')), may hold values from 1 to 128, 256 in all within a row
- attend_gain: bfloat16 [2, 768], P('section', 'dp'), may hold values from 0.5 to 1.5
- attend_bias: bfloat16 [2, 768], P('section', 'dp'), may hold values from -1.5 to 1.5
- qkv_weight: bfloat16 [2, 768, 2304], P('section', 'dp'), may hold values from -0.21875 to 0.21875
- out_weight: bfloat16 [2, 768, 768], P('section', 'dp'), may hold values from -0.875 to 0.875
- feed_gain: bfloat16 [2, 768], P('section', 'dp'), may hold values from 0.5 to 1.5
- feed_bias: bfloat16 [2, 768], P('section', 'dp'), may hold values from -1.5 to 1.5
- up_weight: bfloat16 [2, 768, 3072], P('section', 'dp'), may hold values from -0.21875 to 0.21875
- down_weight: bfloat16 [2, 3072, 768], P('section', 'dp'), may hold values from -0.109375 to 0.109375
Outputs:
- layer_out: bfloat16 [2, 2, 4096, 768], P('section', None, ('group', 'dp'))
- input_grad: bfloat16 [2, 2, 4096, 768], P('section', None, ('group', 'dp'))
- attend_gain_grad: float32 [2, 768], P('section', 'dp')
- attend_bias_grad: float32 [2, 768], P('section', 'dp')
- qkv_grad: float32 [2, 768, 2304], P('section', 'dp')
- out_grad: float32 [2, 768, 768], P('section', 'dp')
- feed_gain_grad: float32 [2, 768], P('section', 'dp')
- feed_bias_grad: float32 [2, 768], P('section', 'dp')
- up_grad: float32 [2, 768, 3072], P('section', 'dp')
- down_grad: float32 [2, 3072, 768], P('section', 'dp')
The draws below stay inside these ranges and needn't reach their ends.
Inputs may be any that keep to these rules, and one draw needn't show every extreme that they name: The 3 lengths of one device's block of a micro-batch add up to 256; the longest sequence of every block has 128 tokens.
All inputs are finite; a program needn't handle non-finite values.
Results may differ from the reference program's by a relative error of at most 0.02.
Values may be sent and summed in bfloat16 or wider, within the bound.
No kernel may reach another device: no remote copies, remote signals or barrier semaphores. Data moves between devices by JAX's collectives and lax.ppermute only.
A program may use at most 192 MiB of HBM per device.

```python
import math
import jax
import jax.numpy as jnp
import numpy as np
from jax import lax

D = 768
HEADS = 12
HEAD_DIM = 64
FF = 3072
TOK_DEV = 256
MICRO = 2
SLOTS = 3
SEQ_MAX = 128
NROWS = 16
TOK_MB = 4096


def steps_of(key, extent, shards, least, high):
    loudness = 1.0
    for dim, shards_of in shards:
        steps = jax.random.uniform(jax.random.fold_in(jax.random.fold_in(key, 6), dim), (shards_of,), jnp.float32, least / len(shards), high / len(shards))
        loudness = loudness * jnp.repeat(jnp.exp(steps), extent[dim] // shards_of).reshape((-1,) + (1,) * (len(extent) - 1 - dim))
    return loudness


def profile(number_of, total, reach, slope):
    portions = [(1 << 20) // math.isqrt(grade ** slope) + 1 for grade in range(2, number_of + 1)]
    spare, counts = total - reach - (number_of - 1), [1] * (number_of - 1)
    while spare > 0:
        free = [i for i in range(number_of - 1) if counts[i] < reach]
        pool, budget = sum([portions[i] for i in free]), spare
        for i in free:
            addition = min(reach - counts[i], max(1, budget * portions[i] // pool), spare)
            counts[i] = counts[i] + addition
            spare = spare - addition
    return np.array([reach] + counts)


def ragged_sizes(rng, count, total, limit, slope):
    if count == 2:
        one = jax.random.randint(rng, (), max(1, total - limit), min(limit, total - 1) + 1)
        return jnp.stack([one, total - one])
    tallies = jnp.asarray(profile(count, total, limit, slope), jnp.int32)
    twos = (count - 1) // 2
    source_of, taker = tallies[1:1 + 2 * twos:2], tallies[2:2 + 2 * twos:2]
    room = jnp.minimum(source_of - 1, limit - taker)
    shifted = jax.random.randint(jax.random.fold_in(rng, 1), (twos,), 0, 1 << 20) % (room + 1)
    tallies = tallies.at[1:1 + 2 * twos:2].set(source_of - shifted).at[2:2 + 2 * twos:2].set(taker + shifted)
    return tallies[jax.random.permutation(jax.random.fold_in(rng, 2), count)]


def scatter_about(key, extent, scale, limit, cuts=(), held_as=jnp.bfloat16):
    values = scale * jax.random.normal(key, extent, jnp.float32)
    if cuts:
        values = values * steps_of(key, extent, cuts, -0.22, 0.18)
    return jnp.clip(values, -limit, limit).astype(held_as)


def setup_inputs(seed: int = 0) -> dict:
    streams_of = jax.random.split(jax.random.key(seed), 12)
    tokens = scatter_about(streams_of[0], (MICRO, TOK_MB, D), 1.0, 6.0, ((1, 16),))
    cotangent = scatter_about(streams_of[1], (MICRO, TOK_MB, D), 1.0, 6.0, ((1, 16),))
    lengths = jax.vmap(lambda own: ragged_sizes(own, SLOTS, TOK_DEV, SEQ_MAX, 2))(jax.random.split(streams_of[2], MICRO * NROWS)).reshape((MICRO, NROWS, SLOTS)).astype(jnp.int32)
    attend_gain = jnp.clip(1.0 + 0.1 * jax.random.normal(streams_of[3], (2, D), jnp.float32), 0.5, 1.5).astype(jnp.bfloat16)
    attend_bias = scatter_about(streams_of[4], (2, D), 0.3, 1.5, ((0, 2), (1, 4)))
    qkv_weight = scatter_about(streams_of[5], (2, D, 3 * D), D ** -0.5, 0.21875, ((0, 2), (1, 4)))
    out_weight = scatter_about(streams_of[6], (2, D, D), (D // 16) ** -0.5, 0.875, ((0, 2), (1, 4)))
    feed_gain = jnp.clip(1.0 + 0.1 * jax.random.normal(streams_of[7], (2, D), jnp.float32), 0.5, 1.5).astype(jnp.bfloat16)
    feed_bias = scatter_about(streams_of[8], (2, D), 0.3, 1.5, ((0, 2), (1, 4)))
    up_weight = scatter_about(streams_of[9], (2, D, FF), D ** -0.5, 0.21875, ((0, 2), (1, 4)))
    down_weight = scatter_about(streams_of[10], (2, FF, D), FF ** -0.5, 0.109375, ((0, 2), (1, 4)))
    return {"tokens": tokens, "cotangent": cotangent, "lengths": lengths, "attend_gain": attend_gain, "attend_bias": attend_bias, "qkv_weight": qkv_weight, "out_weight": out_weight, "feed_gain": feed_gain, "feed_bias": feed_bias, "up_weight": up_weight, "down_weight": down_weight}


@jax.custom_vjp
def low(v):
    return lax.optimization_barrier(v.astype(jnp.bfloat16)).astype(jnp.float32)

@jax.custom_vjp
def low_back(v):
    return v

def low_keep(v):
    return (low(v), None)

def low_pass(kept, grad):
    return (grad,)

def back_keep(v):
    return (v, None)

def back_low(kept, grad):
    return (low(grad),)
low.defvjp(low_keep, low_pass)
low_back.defvjp(back_keep, back_low)
masked_score = -1000000000.0

def rope_tables(lengths_row, tok):
    bounds = jnp.cumsum(lengths_row, dtype=jnp.int32)
    places = jnp.arange(tok, dtype=jnp.int32)
    segment = lax.optimization_barrier(jnp.sum((places[:, None] >= bounds[None, :-1]).astype(jnp.int32), axis=1))
    starts = bounds - lengths_row
    picks = jnp.arange(lengths_row.shape[0], dtype=jnp.int32)
    begin = lax.optimization_barrier(jnp.sum(jnp.where(segment[:, None] == picks[None, :], starts[None, :], 0), axis=1))
    offset = (places - begin).astype(jnp.float32)
    half = HEAD_DIM // 2
    freqs = 10000.0 ** (-jnp.arange(half, dtype=jnp.float32) / half)
    angles = offset[:, None] * freqs[None, :]
    return (jnp.cos(angles), jnp.sin(angles), segment[:, None] == segment[None, :])

def layer_norm(x, gain, bias):
    center = x - lax.optimization_barrier(jnp.mean(x, axis=-1, keepdims=True))
    spread = lax.optimization_barrier(jnp.mean(center * center, axis=-1, keepdims=True))
    return center * lax.rsqrt(spread + 1e-05) * gain + bias

def rotate(heads_in, cosine, sine):
    half = heads_in.shape[-1] // 2
    first = heads_in[..., :half]
    second = heads_in[..., half:]
    cosv = cosine[:, None, :]
    sinv = sine[:, None, :]
    return jnp.concatenate([first * cosv - second * sinv, second * cosv + first * sinv], axis=-1)

def layer(x, params, cosine, sine, same):
    gain_one, bias_one, qkv_w, out_w, gain_two, bias_two, up_w, down_w = params
    high = lax.Precision.HIGHEST
    tok = x.shape[0]
    normed = low(layer_norm(x, gain_one, bias_one))
    qkv = low_back(jnp.dot(normed, qkv_w, precision=high)).reshape(tok, 3, HEADS, HEAD_DIM)
    query = low(rotate(qkv[:, 0], cosine, sine))
    key = low(rotate(qkv[:, 1], cosine, sine))
    value = low(qkv[:, 2])
    scores = jnp.einsum('qhd,khd->hqk', query, key, precision=high) * HEAD_DIM ** (-0.5)
    scores = low_back(jnp.where(same[None], scores, masked_score))
    probs = low(jax.nn.softmax(scores, axis=-1))
    mixed = jnp.einsum('hqk,khd->qhd', probs, value, precision=high).reshape(tok, D)
    mixed = low_back(low(mixed))
    resid = x + low_back(jnp.dot(mixed, out_w, precision=high))
    normed_two = low(layer_norm(resid, gain_two, bias_two))
    upward = low_back(jnp.dot(normed_two, up_w, precision=high))
    active = low(jax.nn.gelu(upward, approximate=False))
    return resid + low_back(jnp.dot(active, down_w, precision=high))

def reference(tokens, cotangent, lengths, attend_gain, attend_bias, qkv_weight, out_weight, feed_gain, feed_bias, up_weight, down_weight):
    blocks = MICRO * NROWS
    group_size = 16 if blocks % 16 == 0 else 1
    count = blocks // group_size
    shape_in = (count, group_size, TOK_DEV, D)
    inputs = tokens.astype(jnp.float32).reshape(shape_in)
    upstream = cotangent.astype(jnp.float32).reshape(shape_in)
    lens = lengths.reshape(blocks, SLOTS)
    cosine, sine, same = jax.vmap(lambda row: rope_tables(row, TOK_DEV))(lens)
    cosine = cosine.reshape(count, group_size, TOK_DEV, HEAD_DIM // 2)
    sine = sine.reshape(count, group_size, TOK_DEV, HEAD_DIM // 2)
    same = same.reshape(count, group_size, TOK_DEV, TOK_DEV)
    weights = (attend_gain, attend_bias, qkv_weight, out_weight, feed_gain, feed_bias, up_weight, down_weight)
    params_a = tuple((w[0].astype(jnp.float32) for w in weights))
    params_b = tuple((w[1].astype(jnp.float32) for w in weights))

    def forward(x_all, probe_all, first_params, second_params):

        def pair(x_blk, probe_blk, cosv, sinv, maskv):
            hidden = layer(x_blk, first_params, cosv, sinv, maskv)
            sent = low_back(low(hidden))
            final = layer(sent + probe_blk, second_params, cosv, sinv, maskv)
            return (low(hidden), final)
        run = jax.checkpoint(jax.vmap(pair))

        def step(carry, item):
            return (carry, run(*item))
        _, outputs = lax.scan(step, None, (x_all, probe_all, cosine, sine, same))
        return outputs
    probe = jnp.zeros_like(inputs)
    (hiddens, finals), pull = jax.vjp(forward, inputs, probe, params_a, params_b)
    d_input, d_probe, grads_a, grads_b = pull((jnp.zeros_like(hiddens), upstream))
    full = (2, MICRO, TOK_MB, D)
    layer_out = jnp.stack([hiddens, finals]).reshape(full).astype(jnp.bfloat16)
    input_grad = jnp.stack([d_input, d_probe]).reshape(full).astype(jnp.bfloat16)
    grads = tuple((jnp.stack([ga, gb]) for ga, gb in zip(grads_a, grads_b)))
    return (layer_out, input_grad, grads[0], grads[1], grads[2], grads[3], grads[4], grads[5], grads[6], grads[7])
```

```python
import functools

import jax
import jax.numpy as jnp
from jax import lax
from jax.experimental import pallas as pl
from jax.experimental.pallas import tpu as pltpu
from jax.sharding import PartitionSpec as P

HEAD_DIM = 64
LANES = 128
BLOCK = 384
PARTS = 4


masked_score = -1000000000.0


def rope_tables(lengths_row, tok):
    bounds = jnp.cumsum(lengths_row, dtype=jnp.int32)
    places = jnp.arange(tok, dtype=jnp.int32)
    segment = jnp.sum((places[:, None] >= bounds[None, :-1]).astype(jnp.int32), axis=1)
    starts = bounds - lengths_row
    picks = jnp.arange(lengths_row.shape[0], dtype=jnp.int32)
    begin = jnp.sum(jnp.where(segment[:, None] == picks[None, :], starts[None, :], 0), axis=1)
    offset = (places - begin).astype(jnp.float32)
    half = HEAD_DIM // 2
    freqs = 10000.0 ** (-jnp.arange(half, dtype=jnp.float32) / half)
    angles = offset[:, None] * freqs[None, :]
    cosine, sine = jnp.cos(angles), jnp.sin(angles)
    heads = LANES // HEAD_DIM
    cosine = jnp.concatenate([cosine, cosine] * heads, axis=1)
    sine = jnp.concatenate([-sine, sine] * heads, axis=1)
    return cosine, sine, segment


def mm(left, right, left_dim, right_dim):
    return lax.dot_general(
        left, right, (((left_dim,), (right_dim,)), ((), ())), preferred_element_type=jnp.float32
    )


def normalize(x):
    center = x - jnp.mean(x, axis=-1, keepdims=True)
    spread = jnp.mean(center * center, axis=-1, keepdims=True)
    scale = lax.rsqrt(spread + 1e-05)
    return center * scale, scale


def norm_backward(d_out, hat, scale, gain):
    d_hat = d_out * gain
    part = d_hat - jnp.mean(d_hat, axis=-1, keepdims=True)
    part = part - hat * jnp.mean(d_hat * hat, axis=-1, keepdims=True)
    return part * scale


def swap_halves(x):
    half = HEAD_DIM // 2
    lane = lax.broadcasted_iota(jnp.int32, x.shape, 1)
    low = lane % HEAD_DIM < half
    return jnp.where(low, pltpu.roll(x, LANES - half, 1), pltpu.roll(x, half, 1))


def head_of(x, which):
    lane = lax.broadcasted_iota(jnp.int32, x.shape, 1)
    inside = lane < HEAD_DIM if which == 0 else lane >= HEAD_DIM
    return jnp.where(inside, x, jnp.zeros_like(x))


def masks_of(groups, low_first):
    bits = [1 << i for i in range(groups.bit_length() - 1)]
    turn = len(bits) // 2
    tables = []
    for order in (bits, bits[turn:] + bits[:turn]):
        if not low_first:
            order = order[::-1]
        tables.append([sum(b for t, b in enumerate(order) if (j >> t) & 1) for j in range(groups)])
    return tables


def pick(flag, a, b):
    return a if a == b else jnp.where(flag, a, b)


class Plan:
    def __init__(self, groups, rows, tok, width):
        self.groups = groups
        self.rows = rows
        self.tok = tok
        self.width = width
        self.pieces = groups * rows
        self.tall = width // self.pieces
        self.direct = self.tall % 16 == 0


def start_weights(plan, layer, kind, ids, own, others, whole, dst, sem):
    width, tall = plan.width, plan.tall
    if not plan.direct:
        for h in range(2):
            lanes = pl.ds(h * BLOCK, BLOCK)
            if kind == "down":
                pltpu.make_async_copy(whole.at[h], dst.at[:, lanes], sem).start()
            else:
                pltpu.make_async_copy(whole.at[h], dst.at[:, :, lanes], sem).start()
        return
    core, group, row = ids[0], ids[1], ids[2]
    share = width // plan.rows
    mine, theirs = own

    def from_shard(refs):
        if kind == "down":
            at = pl.multiple_of(row * (share * PARTS), 16)
            pltpu.make_async_copy(refs[0].at[0], dst.at[pl.ds(at, share * PARTS)], sem).start()
            return
        at = pl.multiple_of(row * share, 16)
        j = 0
        for ref in refs:
            for b in range(ref.shape[2] // width):
                pltpu.make_async_copy(
                    ref.at[0, :, pl.ds(b * width, width)], dst.at[j, pl.ds(at, share)], sem
                ).start()
                j += 1

    @pl.when(core == layer)
    def _():
        from_shard(mine)

    @pl.when(core != layer)
    def _():
        from_shard(theirs)

    tables = masks_of(plan.groups, True)
    for source, flag in zip(others, (core == 0, core != 0)):
        half = core if source is others[0] else 1 - core
        lanes = pl.ds(pl.multiple_of(half * BLOCK, LANES), BLOCK)
        for j in range(plan.groups):
            peer = group ^ pick(flag, tables[0][j], tables[1][j])
            for k in range(plan.rows - 1):
                at = ((row + (plan.rows - 1 - k)) % plan.rows) * plan.groups + peer
                if kind == "down":
                    at = pl.multiple_of(at * (tall * PARTS), 16)
                    to = dst.at[pl.ds(at, tall * PARTS), lanes]
                else:
                    to = dst.at[:, pl.ds(pl.multiple_of(at * tall, 16), tall), lanes]
                pltpu.make_async_copy(source.at[j, k], to, sem).start()


def wait_all(ref, sem):
    pltpu.make_async_copy(ref, ref, sem).wait()


def start_grads(plan, kind, ids, src, keep, send, sem):
    width, tall = plan.width, plan.tall
    core, group, row = ids[0], ids[1], ids[2]
    if not plan.direct:
        for out, half in ((keep, core), (send, 1 - core)):
            lanes = pl.ds(pl.multiple_of(half * BLOCK, LANES), BLOCK)
            if kind == "down":
                pltpu.make_async_copy(src.at[:, lanes], out, sem).start()
            else:
                pltpu.make_async_copy(src.at[:, :, lanes], out, sem).start()
        return
    tables = masks_of(plan.groups, False)
    for out, half, flag in ((keep, core, core == 0), (send, 1 - core, core != 0)):
        lanes = pl.ds(pl.multiple_of(half * BLOCK, LANES), BLOCK)
        for j in range(plan.groups):
            peer = group ^ pick(flag, tables[0][j], tables[1][j])
            for k in range(plan.rows):
                at = ((row + k) % plan.rows) * plan.groups + peer
                if kind == "down":
                    part = src.at[pl.ds(pl.multiple_of(at * (tall * PARTS), 16), tall * PARTS), lanes]
                else:
                    part = src.at[:, pl.ds(pl.multiple_of(at * tall, 16), tall), lanes]
                pltpu.make_async_copy(part, out.at[j, k], sem).start()


def attend_forward(plan, layer, ids, lens, x_ref, small, cosv, sinv, *refs):
    n = 7
    own, others, whole = weight_refs(plan, "attend", refs[: plan_inputs(plan, "attend")])
    refs = refs[plan_inputs(plan, "attend") :]
    normed, qkv, probs, mixed, resid, w, same, sem = refs
    width, tok = plan.width, plan.tok
    start_weights(plan, layer, "attend", ids, own, others, whole, w, sem)
    x = x_ref[...].astype(jnp.float32)
    hat, _ = normalize(x)
    low = (hat * small[0:1, :] + small[1:2, :]).astype(jnp.bfloat16)
    normed[...] = low
    first_end = lens[0]
    second_end = lens[0] + lens[1]

    def seg(axis):
        at = lax.broadcasted_iota(jnp.int32, (tok, tok), axis)
        return (at >= first_end).astype(jnp.int32) + (at >= second_end).astype(jnp.int32)

    same[...] = (seg(0) == seg(1)).astype(jnp.float32)
    wait_all(w, sem)
    for j in range(3):
        full = mm(low, w[j], 1, 0)
        if j == 2:
            qkv[:, j * width : (j + 1) * width] = full.astype(jnp.bfloat16)
            continue
        for t in range(width // LANES):
            part = full[:, t * LANES : (t + 1) * LANES]
            part = part * cosv[...] + swap_halves(part) * sinv[...]
            qkv[:, j * width + t * LANES : j * width + (t + 1) * LANES] = part.astype(jnp.bfloat16)

    def tile(t, carry):
        at = pl.multiple_of(t * LANES, LANES)
        q = qkv[:, pl.ds(at, LANES)]
        k = qkv[:, pl.ds(width + at, LANES)]
        v = qkv[:, pl.ds(2 * width + at, LANES)]
        total = None
        for h in range(2):
            scores = mm(head_of(q, h), k, 1, 1) * HEAD_DIM ** (-0.5)
            scores = jnp.where(same[...] > 0.5, scores, masked_score)
            peak = jnp.max(scores, axis=-1, keepdims=True)
            expd = jnp.exp(scores - peak)
            p = expd * (1.0 / jnp.sum(expd, axis=-1, keepdims=True))
            probs[2 * t + h] = p
            part = mm(p.astype(jnp.bfloat16), head_of(v, h), 1, 0)
            total = part if total is None else total + part
        mixed[:, pl.ds(at, LANES)] = total.astype(jnp.bfloat16)
        return carry

    lax.fori_loop(0, width // LANES, tile, 0)
    resid[...] = x + mm(mixed[...], w[3], 1, 0)


def feed_forward(plan, layer, ids, resid, small, *refs):
    a = plan_inputs(plan, "up")
    b = plan_inputs(plan, "down")
    up_refs = weight_refs(plan, "up", refs[:a])
    down_refs = weight_refs(plan, "down", refs[a : a + b])
    normed, active, slope, y, wu, wd, sem_u, sem_d = refs[a + b :]
    width = plan.width
    start_weights(plan, layer, "up", ids, *up_refs, wu, sem_u)
    start_weights(plan, layer, "down", ids, *down_refs, wd, sem_d)
    hat, _ = normalize(resid[...])
    low = (hat * small[2:3, :] + small[3:4, :]).astype(jnp.bfloat16)
    normed[...] = low
    wait_all(wu, sem_u)
    total = resid[...]
    for j in range(PARTS):
        v = mm(low, wu[j], 1, 0)
        cdf = 0.5 * (1.0 + lax.erf(v * (2.0**-0.5)))
        act = (v * cdf).astype(jnp.bfloat16)
        lanes = slice(j * width, (j + 1) * width)
        active[:, lanes] = act
        slope[:, lanes] = cdf + v * (jnp.exp(v * v * -0.5) * 0.3989422804014327)
        if j == 0:
            wait_all(wd, sem_d)
        total = total + mm(act, wd[lanes, :], 1, 0)
    y[...] = total.astype(jnp.bfloat16)


def down_grad(plan, ids, active, d_out, keep, send, g, sem):
    width = plan.width
    d = d_out[...]
    for j in range(PARTS):
        g[j * width : (j + 1) * width, :] = mm(
            active[:, j * width : (j + 1) * width], d, 0, 0
        ).astype(jnp.bfloat16)
    start_grads(plan, "down", ids, g, keep, send, sem)
    wait_all(g, sem)


def feed_backward(plan, layer, ids, d_out, resid, normed, slope, small, *refs):
    a = plan_inputs(plan, "up")
    b = plan_inputs(plan, "down")
    up_refs = weight_refs(plan, "up", refs[:a])
    down_refs = weight_refs(plan, "down", refs[a : a + b])
    keep, send, d_resid, sums, wu, wd, g, sem_u, sem_d, sem_g = refs[a + b :]
    width = plan.width
    start_weights(plan, layer, "down", ids, *down_refs, wd, sem_d)
    start_weights(plan, layer, "up", ids, *up_refs, wu, sem_u)
    d = d_out[...]
    low = normed[...]
    wait_all(wd, sem_d)
    total = None
    for j in range(PARTS):
        lanes = slice(j * width, (j + 1) * width)
        d_up = (mm(d, wd[lanes, :], 1, 1) * slope[:, lanes]).astype(jnp.bfloat16)
        g[j] = mm(low, d_up, 0, 0).astype(jnp.bfloat16)
        if j == 0:
            wait_all(wu, sem_u)
        part = mm(d_up, wu[j], 1, 1)
        total = part if total is None else total + part
    start_grads(plan, "up", ids, g, keep, send, sem_g)
    hat, scale = normalize(resid[...])
    sums[0:1, :] = jnp.sum(total * hat, axis=0, keepdims=True)
    sums[1:2, :] = jnp.sum(total, axis=0, keepdims=True)
    d_resid[...] = d.astype(jnp.float32) + norm_backward(total, hat, scale, small[2:3, :])
    wait_all(g, sem_g)


def attend_backward(plan, layer, ids, x_ref, d_resid, normed, qkv, probs, mixed, small, cosv, sinv, *refs):
    a = plan_inputs(plan, "attend")
    own, others, whole = weight_refs(plan, "attend", refs[:a])
    keep, send, dx, sums, w, g, d_mixed, d_qkv, sem_w, sem_g = refs[a:]
    width = plan.width
    start_weights(plan, layer, "attend", ids, own, others, whole, w, sem_w)
    d = d_resid[...].astype(jnp.bfloat16)
    g[3] = mm(mixed[...], d, 0, 0).astype(jnp.bfloat16)
    wait_all(w, sem_w)
    d_mixed[...] = mm(d, w[3], 1, 1).astype(jnp.bfloat16)

    def tile(t, carry):
        at = pl.multiple_of(t * LANES, LANES)
        q = qkv[:, pl.ds(at, LANES)]
        k = qkv[:, pl.ds(width + at, LANES)]
        v = qkv[:, pl.ds(2 * width + at, LANES)]
        dm = d_mixed[:, pl.ds(at, LANES)]
        dq = dk = dv = None
        for h in range(2):
            p = probs[2 * t + h]
            dm_h = head_of(dm, h)
            dv_h = mm(p.astype(jnp.bfloat16), dm_h, 0, 0)
            dp = mm(dm_h, v, 1, 1)
            ds = p * (dp - jnp.sum(dp * p, axis=-1, keepdims=True))
            ds = ds.astype(jnp.bfloat16)
            dq_h = mm(ds, head_of(k, h), 1, 0)
            dk_h = mm(ds, head_of(q, h), 0, 0)
            dq = dq_h if dq is None else dq + dq_h
            dk = dk_h if dk is None else dk + dk_h
            dv = dv_h if dv is None else dv + dv_h
        scale = HEAD_DIM ** (-0.5)
        dq = dq * scale
        dk = dk * scale
        dq = dq * cosv[...] - swap_halves(dq) * sinv[...]
        dk = dk * cosv[...] - swap_halves(dk) * sinv[...]
        d_qkv[:, pl.ds(at, LANES)] = dq.astype(jnp.bfloat16)
        d_qkv[:, pl.ds(width + at, LANES)] = dk.astype(jnp.bfloat16)
        d_qkv[:, pl.ds(2 * width + at, LANES)] = dv.astype(jnp.bfloat16)
        return carry

    lax.fori_loop(0, width // LANES, tile, 0)
    low = normed[...]
    total = None
    for j in range(3):
        part_in = d_qkv[:, j * width : (j + 1) * width]
        g[j] = mm(low, part_in, 0, 0).astype(jnp.bfloat16)
        part = mm(part_in, w[j], 1, 1)
        total = part if total is None else total + part
    start_grads(plan, "attend", ids, g, keep, send, sem_g)
    hat, scale = normalize(x_ref[...].astype(jnp.float32))
    sums[0:1, :] = jnp.sum(total * hat, axis=0, keepdims=True)
    sums[1:2, :] = jnp.sum(total, axis=0, keepdims=True)
    back = d_resid[...] + norm_backward(total, hat, scale, small[0:1, :])
    dx[...] = back.astype(jnp.bfloat16)
    wait_all(g, sem_g)


SHARDS = {"attend": 2, "up": 1, "down": 1}


def plan_inputs(plan, kind):
    return 2 * SHARDS[kind] + 2 if plan.direct else 1


def weight_refs(plan, kind, refs):
    if not plan.direct:
        return None, None, refs[0]
    n = SHARDS[kind]
    return (refs[:n], refs[n : 2 * n]), refs[2 * n :], None


VMEM = pl.BlockSpec(memory_space=pltpu.VMEM)
SMEM = pl.BlockSpec(memory_space=pltpu.SMEM)
HBM = pl.BlockSpec(memory_space=pl.ANY)


def call(body, name, args, specs, outs, out_specs, scratch, flops):
    moved = sum(x.size * x.dtype.itemsize for x in list(args) + list(outs))
    return pl.pallas_call(
        body,
        out_shape=outs,
        in_specs=specs,
        out_specs=out_specs,
        scratch_shapes=scratch,
        name=name,
        cost_estimate=pl.CostEstimate(flops=flops, transcendentals=0, bytes_accessed=moved),
        compiler_params=pltpu.CompilerParams(vmem_limit_bytes=58 << 20),
    )(*args)


def shape(dims, dtype):
    return jax.ShapeDtypeStruct(dims, dtype)


BF, F32 = jnp.bfloat16, jnp.float32


class Kernels:
    def __init__(self, plan, ids, lens, tables, heads):
        self.plan, self.ids, self.lens, self.tables, self.heads = plan, ids, lens, tables, heads
        self.part = pltpu.VMEM((PARTS, plan.width, plan.width), BF)
        self.tall = pltpu.VMEM((PARTS * plan.width, plan.width), BF)
        self.sem = pltpu.SemaphoreType.DMA(())

    def attend_forward(self, layer, x, small, weights):
        p = self.plan
        t, d = p.tok, p.width
        return call(
            functools.partial(attend_forward, p, layer),
            f"attend_forward_{layer}",
            (self.ids, self.lens, x, small, *self.tables, *weights),
            [SMEM, SMEM] + [VMEM] * 4 + [HBM] * len(weights),
            (
                shape((t, d), BF),
                shape((t, 3 * d), BF),
                shape((self.heads, t, t), F32),
                shape((t, d), BF),
                shape((t, d), F32),
            ),
            (VMEM,) * 5,
            [self.part, pltpu.VMEM((t, t), F32), self.sem],
            2 * t * d * d * 4 + 4 * self.heads * t * t * LANES,
        )

    def feed_forward(self, layer, resid, small, weights):
        p = self.plan
        t, d = p.tok, p.width
        return call(
            functools.partial(feed_forward, p, layer),
            f"feed_forward_{layer}",
            (self.ids, resid, small, *weights),
            [SMEM, VMEM, VMEM] + [HBM] * len(weights),
            (
                shape((t, d), BF),
                shape((t, PARTS * d), BF),
                shape((t, PARTS * d), F32),
                shape((t, d), BF),
            ),
            (VMEM,) * 4,
            [self.part, self.tall, self.sem, self.sem],
            2 * t * d * d * 8,
        )

    def grads(self, kind):
        p = self.plan
        rows = p.tall * PARTS if kind == "down" else None
        if not p.direct:
            dims = (PARTS * p.width, BLOCK) if kind == "down" else (PARTS, p.width, BLOCK)
        elif kind == "down":
            dims = (p.groups, p.rows, rows, BLOCK)
        else:
            dims = (p.groups, p.rows, PARTS, p.tall, BLOCK)
        return (shape(dims, BF), shape(dims, BF))

    def down_grad(self, layer, active, d_out):
        p = self.plan
        return call(
            functools.partial(down_grad, p),
            f"down_grad_{layer}",
            (self.ids, active, d_out),
            [SMEM, VMEM, VMEM],
            self.grads("down"),
            (HBM, HBM),
            [self.tall, self.sem],
            2 * p.tok * p.width * p.width * 4,
        )

    def feed_backward(self, layer, d_out, resid, normed, slope, small, weights):
        p = self.plan
        t, d = p.tok, p.width
        return call(
            functools.partial(feed_backward, p, layer),
            f"feed_backward_{layer}",
            (self.ids, d_out, resid, normed, slope, small, *weights),
            [SMEM] + [VMEM] * 5 + [HBM] * len(weights),
            (*self.grads("up"), shape((t, d), F32), shape((2, d), F32)),
            (HBM, HBM, VMEM, VMEM),
            [self.part, self.tall, self.part, self.sem, self.sem, self.sem],
            2 * t * d * d * 12,
        )

    def attend_backward(self, layer, x, d_resid, normed, qkv, probs, mixed, small, weights):
        p = self.plan
        t, d = p.tok, p.width
        return call(
            functools.partial(attend_backward, p, layer),
            f"attend_backward_{layer}",
            (self.ids, x, d_resid, normed, qkv, probs, mixed, small, *self.tables, *weights),
            [SMEM] + [VMEM] * 9 + [HBM] * len(weights),
            (*self.grads("attend"), shape((t, d), BF), shape((2, d), F32)),
            (HBM, HBM, VMEM, VMEM),
            [self.part, self.part, pltpu.VMEM((t, d), BF), pltpu.VMEM((t, 3 * d), BF), self.sem, self.sem],
            2 * t * d * d * 8 + 10 * self.heads * t * t * LANES,
        )


def swap_cores(x):
    return lax.ppermute(x, "section", [(0, 1), (1, 0)])


def stage_bits(groups):
    bits = [1 << i for i in range(groups.bit_length() - 1)]
    turn = len(bits) // 2
    return bits, bits[turn:] + bits[:turn]


def swap_groups(x, groups, stage):
    pairs = []
    for core, bits in enumerate(stage_bits(groups)):
        pairs += [(core * groups + g, core * groups + (g ^ bits[stage])) for g in range(groups)]
    return lax.ppermute(x, ("section", "group"), pairs)


def along(x, distance):
    rows = lax.axis_size("dp")
    return lax.ppermute(x, "dp", [(i, (i + distance) % rows) for i in range(rows)])


def gate(x, after):
    return lax.optimization_barrier((x, *after))[0] if after else x


KINDS = ("attend", "up", "down")


def piece_of(plan, group, kind, shards):
    tall = plan.tall

    def cut(w, inside):
        if inside:
            w = lax.dynamic_slice_in_dim(w[0], group * (tall * PARTS), tall * PARTS, 0)
            return w.reshape(PARTS, tall, 2, BLOCK).transpose(2, 0, 1, 3)
        w = lax.dynamic_slice_in_dim(w[0], group * tall, tall, 0)
        return w.reshape(tall, -1, 2, BLOCK).transpose(2, 1, 0, 3)

    return jnp.concatenate([cut(w, kind == "down") for w in shards], axis=1)


def whole_of(plan, core, group, row, kind, shard, half_mine, half_theirs):
    groups, rows, tall = plan.groups, plan.rows, plan.tall
    tables = jnp.array(masks_of(groups, True), jnp.int32)
    first = core == 0
    halves = []
    for h in range(2):
        got = jnp.where(core == h, half_mine, half_theirs)
        got = jnp.take(got, jnp.argsort(group ^ tables[h]), axis=0)
        own = []
        for w in shard:
            if kind == "down":
                w = w[0].reshape(groups, PARTS, tall, 2, BLOCK)[:, :, :, h]
            else:
                w = w[0].reshape(groups, tall, -1, 2, BLOCK)[:, :, :, h].transpose(0, 2, 1, 3)
            own.append(w)
        own = jnp.concatenate(own, axis=1)[:, None]
        got = jnp.concatenate([got, own], axis=1)
        got = jnp.take(got, (row - 1 - jnp.arange(rows)) % rows, axis=1)
        if kind == "down":
            halves.append(got.transpose(1, 0, 2, 3, 4).reshape(PARTS * plan.width, BLOCK))
        else:
            halves.append(got.transpose(2, 1, 0, 3, 4).reshape(PARTS, plan.width, BLOCK))
    return jnp.stack(halves)


def ordered_grads(plan, kind, core, group, row, keep, send):
    groups, rows, tall = plan.groups, plan.rows, plan.tall
    tables = jnp.array(masks_of(groups, False), jnp.int32)
    outs = []
    for x, half in ((keep, core), (send, 1 - core)):
        if kind == "down":
            x = x.reshape(rows, groups, PARTS, tall, BLOCK).transpose(1, 0, 2, 3, 4)
        else:
            x = x.reshape(PARTS, rows, groups, tall, BLOCK).transpose(2, 1, 0, 3, 4)
        x = jnp.take(x, group ^ jnp.where(half == 0, tables[0], tables[1]), axis=0)
        x = jnp.take(x, (row + jnp.arange(rows)) % rows, axis=1)
        outs.append(x)
    return outs


def on_device(
    tokens,
    cotangent,
    lengths,
    attend_gain,
    attend_bias,
    qkv_weight,
    out_weight,
    feed_gain,
    feed_bias,
    up_weight,
    down_weight,
):
    core = lax.axis_index("section")
    group = lax.axis_index("group")
    row = lax.axis_index("dp")
    groups = lax.axis_size("group")
    rows = lax.axis_size("dp")
    stages = groups.bit_length() - 1
    tok, width = tokens.shape[1:]
    plan = Plan(groups, rows, tok, width)
    few = rows <= 4
    first = core == 0
    share = width // rows
    ids = jnp.stack([core, group, row]).astype(jnp.int32)
    lens = lax.dynamic_index_in_dim(lengths, core, 0, False)[0]

    shards = {"attend": (qkv_weight, out_weight), "up": (up_weight,), "down": (down_weight,)}
    pieces = {}
    for kind in KINDS:
        both = piece_of(plan, group, kind, shards[kind])
        keep = lax.dynamic_index_in_dim(both, core, 0, False)
        got = swap_cores(lax.dynamic_index_in_dim(both, 1 - core, 0, False))
        pieces[0, kind] = jnp.where(first, keep, got)
        pieces[1, kind] = jnp.where(first, got, keep)
    theirs = {}
    chunks = [(layer, kind) for layer in range(2) for kind in KINDS]
    history = []
    bufs = {}
    for slot in range(len(chunks) + stages):
        after = history[slot - DEPTH] if slot >= DEPTH else []
        done = []
        for stage in range(stages, 0, -1):
            c = slot - stage
            if 0 <= c < len(chunks):
                got = swap_groups(gate(bufs[c], after), groups, stage - 1)
                bufs[c] = jnp.concatenate([bufs[c], got], axis=0)
                done.append(got)
        if slot < len(chunks):
            piece = gate(pieces[chunks[slot]], after)
            if few:
                got = [along(piece, k) for k in range(1, rows)]
                bufs[slot] = jnp.stack(got)[None]
            else:
                got = [lax.all_gather(piece, "dp")]
                back = (row - 1 - jnp.arange(rows - 1)) % rows
                bufs[slot] = jnp.take(got[0], back, axis=0)[None]
            done += got
        if slot == 0:
            small = jnp.stack([attend_gain[0], attend_bias[0], feed_gain[0], feed_bias[0]])
            smalls = lax.all_gather(gate(small, done[:1]), ("section", "dp"))
            smalls = smalls.reshape(2, rows, PARTS, share).transpose(0, 2, 1, 3)
            smalls = smalls.reshape(2, PARTS, width).astype(F32)
        if slot == 1:
            for kind in KINDS:
                theirs[kind] = tuple(swap_cores(gate(w, done[:1])) for w in shards[kind])
        history.append(done)
    gathered = {}
    for c, (layer, kind) in enumerate(chunks):
        mine = bufs[c]
        other = swap_cores(mine)
        if plan.direct:
            if kind == "down":
                flat = (groups, rows - 1, PARTS * plan.tall, BLOCK)
                mine, other = mine.reshape(flat), other.reshape(flat)
            gathered[layer, kind] = (*shards[kind], *theirs[kind], mine, other)
        else:
            shard = [jnp.where(core == layer, a, b) for a, b in zip(shards[kind], theirs[kind])]
            gathered[layer, kind] = (
                whole_of(plan, core, group, row, kind, shard, mine, other),
            )

    x0 = lax.dynamic_index_in_dim(tokens, core, 0, False)
    cot = lax.dynamic_index_in_dim(cotangent, core, 0, False)
    cosine, sine, _ = rope_tables(lens, tok)
    kernels = Kernels(plan, ids, lens, (cosine, sine), width // HEAD_DIM)
    xs, saved = [x0], []
    for layer in range(2):
        a = kernels.attend_forward(layer, xs[layer], smalls[layer], gathered[layer, "attend"])
        weights = gathered[layer, "up"] + gathered[layer, "down"]
        f = kernels.feed_forward(layer, a[4], smalls[layer], weights)
        xs.append(f[3])
        saved.append((a, f))
    grads, sums, backs = {}, {}, [None, None]
    d_out = cot
    for layer in (1, 0):
        (normed, qkv, probs, mixed, resid), (normed_two, active, slope, _) = saved[layer]
        grads[layer, "down"] = kernels.down_grad(layer, active, d_out)
        weights = gathered[layer, "up"] + gathered[layer, "down"]
        *g, d_resid, sums_two = kernels.feed_backward(
            layer, d_out, resid, normed_two, slope, smalls[layer], weights
        )
        grads[layer, "up"] = g
        *g, d_out, sums_one = kernels.attend_backward(
            layer, xs[layer], d_resid, normed, qkv, probs, mixed, smalls[layer], gathered[layer, "attend"]
        )
        grads[layer, "attend"] = g
        sums[layer] = jnp.concatenate([sums_one, sums_two])
        backs[layer] = d_out

    def home(low, high):
        got = swap_cores(jnp.where(first, high, low))
        keep = jnp.where(first, low, high)
        return jnp.where(first, jnp.stack([keep, got]), jnp.stack([got, keep]))

    layer_out = home(xs[1], xs[2])
    input_grad = home(*backs)

    def add(a, b):
        return (a.astype(F32) + b.astype(F32)).astype(BF)

    def reduce(kind, keep, send):
        if plan.direct:
            dims = (groups, rows, PARTS, plan.tall, BLOCK)
            keep, send = keep.reshape(dims), send.reshape(dims)
        else:
            keep, send = ordered_grads(plan, kind, core, group, row, keep, send)
        got = swap_cores(send)
        for stage in range(stages):
            half = keep.shape[0] // 2
            high = add(keep[half:], got[half:])
            keep = add(keep[:half], got[:half])
            got = swap_groups(high, groups, stage)
        keep, got = keep[0], got[0]
        if few:
            moved = [along(add(keep[k], got[k]), k) for k in range(1, rows)]
            total = keep[0].astype(F32) + got[0].astype(F32)
            for m in moved:
                total = total + m.astype(F32)
        else:
            total = add(keep, got)
            total = jnp.take(total, (jnp.arange(rows) - row) % rows, axis=0)
            total = lax.psum_scatter(total, "dp", scatter_dimension=0, tiled=False)
        total = total.astype(BF)[None]
        for stage in range(stages - 1, -1, -1):
            total = jnp.concatenate([total, swap_groups(total, groups, stage)], axis=0)
        return total

    reduced = {}
    for layer in (1, 0):
        for kind in ("down", "up", "attend"):
            reduced[layer, kind] = reduce(kind, *grads[layer, kind])
    tables = jnp.array(masks_of(groups, False), jnp.int32)
    final = {}
    for kind in KINDS:
        own = jnp.where(first, reduced[0, kind], reduced[1, kind])
        other = swap_cores(jnp.where(first, reduced[1, kind], reduced[0, kind]))
        low = jnp.where(first, own, other)
        high = jnp.where(first, other, own)
        low = jnp.take(low, jnp.argsort(group ^ tables[0]), axis=0)
        high = jnp.take(high, jnp.argsort(group ^ tables[1]), axis=0)
        final[kind] = jnp.stack([low, high])

    def outside(x):
        return x.transpose(1, 3, 2, 0, 4).reshape(share, -1).astype(F32)

    qkv_grad = outside(final["attend"][:, :, 0:3])
    out_grad = outside(final["attend"][:, :, 3:4])
    up_grad = outside(final["up"])
    down_grads = final["down"].transpose(1, 2, 3, 0, 4).reshape(-1, width).astype(F32)

    small_grads = jnp.stack([sums[0], sums[1]])
    small_grads = lax.psum(small_grads, ("section", "group", "dp"))
    own = lax.dynamic_index_in_dim(small_grads, core, 0, False)
    own = lax.dynamic_slice_in_dim(own, row * share, share, 1)
    return (
        layer_out[None],
        input_grad[None],
        own[0][None],
        own[1][None],
        qkv_grad[None],
        out_grad[None],
        own[2][None],
        own[3][None],
        up_grad[None],
        down_grads[None],
    )


DEPTH = 2


def solution(mesh):
    placed = (
        P(None, ("group", "dp"), None),
        P(None, ("group", "dp"), None),
        P(None, ("group", "dp"), None),
        P("section", "dp"),
        P("section", "dp"),
        P("section", "dp", None),
        P("section", "dp", None),
        P("section", "dp"),
        P("section", "dp"),
        P("section", "dp", None),
        P("section", "dp", None),
    )
    return jax.shard_map(
        on_device,
        mesh=mesh,
        in_specs=placed,
        out_specs=(
            P("section", None, ("group", "dp"), None),
            P("section", None, ("group", "dp"), None),
            P("section", "dp"),
            P("section", "dp"),
            P("section", "dp", None),
            P("section", "dp", None),
            P("section", "dp"),
            P("section", "dp"),
            P("section", "dp", None),
            P("section", "dp", None),
        ),
        check_vma=False,
    )
```

```python
import functools

import jax
import jax.numpy as jnp
from jax import lax
from jax.experimental import pallas as pl
from jax.experimental.pallas import tpu as pltpu
from jax.sharding import PartitionSpec as P

HEAD_DIM = 64
LANES = 128
BLOCK = 384
PARTS = 4


masked_score = -1000000000.0


def rope_tables(lengths_row, tok):
    bounds = jnp.cumsum(lengths_row, dtype=jnp.int32)
    places = jnp.arange(tok, dtype=jnp.int32)
    segment = jnp.sum((places[:, None] >= bounds[None, :-1]).astype(jnp.int32), axis=1)
    starts = bounds - lengths_row
    picks = jnp.arange(lengths_row.shape[0], dtype=jnp.int32)
    begin = jnp.sum(jnp.where(segment[:, None] == picks[None, :], starts[None, :], 0), axis=1)
    offset = (places - begin).astype(jnp.float32)
    half = HEAD_DIM // 2
    freqs = 10000.0 ** (-jnp.arange(half, dtype=jnp.float32) / half)
    angles = offset[:, None] * freqs[None, :]
    cosine, sine = jnp.cos(angles), jnp.sin(angles)
    heads = LANES // HEAD_DIM
    cosine = jnp.concatenate([cosine, cosine] * heads, axis=1)
    sine = jnp.concatenate([-sine, sine] * heads, axis=1)
    return cosine, sine, segment


def mm(left, right, left_dim, right_dim):
    return lax.dot_general(
        left, right, (((left_dim,), (right_dim,)), ((), ())), preferred_element_type=jnp.float32
    )


def normalize(x):
    center = x - jnp.mean(x, axis=-1, keepdims=True)
    spread = jnp.mean(center * center, axis=-1, keepdims=True)
    scale = lax.rsqrt(spread + 1e-05)
    return center * scale, scale


def norm_backward(d_out, hat, scale, gain):
    d_hat = d_out * gain
    part = d_hat - jnp.mean(d_hat, axis=-1, keepdims=True)
    part = part - hat * jnp.mean(d_hat * hat, axis=-1, keepdims=True)
    return part * scale


def swap_halves(x):
    half = HEAD_DIM // 2
    lane = lax.broadcasted_iota(jnp.int32, x.shape, 1)
    low = lane % HEAD_DIM < half
    return jnp.where(low, pltpu.roll(x, LANES - half, 1), pltpu.roll(x, half, 1))


def head_of(x, which):
    lane = lax.broadcasted_iota(jnp.int32, x.shape, 1)
    inside = lane < HEAD_DIM if which == 0 else lane >= HEAD_DIM
    return jnp.where(inside, x, jnp.zeros_like(x))


def masks_of(groups, low_first):
    bits = [1 << i for i in range(groups.bit_length() - 1)]
    turn = len(bits) // 2
    tables = []
    for order in (bits, bits[turn:] + bits[:turn]):
        if not low_first:
            order = order[::-1]
        tables.append([sum(b for t, b in enumerate(order) if (j >> t) & 1) for j in range(groups)])
    return tables


def row_masks(rows):
    bits = [1 << i for i in reversed(range(rows.bit_length() - 1))]
    return [sum(b for t, b in enumerate(bits) if (k >> t) & 1) for k in range(rows)]


def row_to(plan, row, k):
    return row ^ row_masks(plan.rows)[k] if plan.few else (row + k) % plan.rows


def row_from(plan, row, k):
    if plan.few:
        return row ^ row_masks(plan.rows)[k + 1]
    return (row + (plan.rows - 1 - k)) % plan.rows


def pick(flag, a, b):
    return a if a == b else jnp.where(flag, a, b)


class Plan:
    def __init__(self, groups, rows, tok, width):
        self.groups = groups
        self.rows = rows
        self.tok = tok
        self.width = width
        self.pieces = groups * rows
        self.tall = width // self.pieces
        self.direct = self.tall % 16 == 0
        self.few = rows <= 4 and rows & (rows - 1) == 0


def start_weights(plan, layer, kind, ids, own, others, whole, dst, sem):
    width, tall = plan.width, plan.tall
    if not plan.direct:
        for h in range(2):
            lanes = pl.ds(h * BLOCK, BLOCK)
            if kind == "down":
                pltpu.make_async_copy(whole.at[h], dst.at[:, lanes], sem).start()
            else:
                pltpu.make_async_copy(whole.at[h], dst.at[:, :, lanes], sem).start()
        return
    core, group, row = ids[0], ids[1], ids[2]
    share = width // plan.rows
    mine, theirs = own

    def from_shard(refs):
        if kind == "down":
            at = pl.multiple_of(row * (share * PARTS), 16)
            pltpu.make_async_copy(refs[0].at[0], dst.at[pl.ds(at, share * PARTS)], sem).start()
            return
        at = pl.multiple_of(row * share, 16)
        j = 0
        for ref in refs:
            for b in range(ref.shape[2] // width):
                pltpu.make_async_copy(
                    ref.at[0, :, pl.ds(b * width, width)], dst.at[j, pl.ds(at, share)], sem
                ).start()
                j += 1

    @pl.when(core == layer)
    def _():
        from_shard(mine)

    @pl.when(core != layer)
    def _():
        from_shard(theirs)

    tables = masks_of(plan.groups, True)
    for half, flag, sources in ((core, core == 0, others[:2]), (1 - core, core != 0, others[2:])):
        lanes = pl.ds(pl.multiple_of(half * BLOCK, LANES), BLOCK)
        for j in range(plan.groups):
            peer = group ^ pick(flag, tables[0][j], tables[1][j])
            source = sources[j // (plan.groups // 2)]
            for k in range(plan.rows - 1):
                at = row_from(plan, row, k) * plan.groups + peer
                if kind == "down":
                    at = pl.multiple_of(at * (tall * PARTS), 16)
                    to = dst.at[pl.ds(at, tall * PARTS), lanes]
                else:
                    to = dst.at[:, pl.ds(pl.multiple_of(at * tall, 16), tall), lanes]
                pltpu.make_async_copy(source.at[j % (plan.groups // 2), k], to, sem).start()


def wait_all(ref, sem):
    pltpu.make_async_copy(ref, ref, sem).wait()


def start_grads(plan, kind, ids, src, keep, send, sem):
    width, tall = plan.width, plan.tall
    core, group, row = ids[0], ids[1], ids[2]
    if not plan.direct:
        for out, half in ((keep, core), (send, 1 - core)):
            lanes = pl.ds(pl.multiple_of(half * BLOCK, LANES), BLOCK)
            if kind == "down":
                pltpu.make_async_copy(src.at[:, lanes], out, sem).start()
            else:
                pltpu.make_async_copy(src.at[:, :, lanes], out, sem).start()
        return
    tables = masks_of(plan.groups, False)
    for out, half, flag in ((keep, core, core == 0), (send, 1 - core, core != 0)):
        lanes = pl.ds(pl.multiple_of(half * BLOCK, LANES), BLOCK)
        for j in range(plan.groups):
            peer = group ^ pick(flag, tables[0][j], tables[1][j])
            for k in range(plan.rows):
                at = row_to(plan, row, k) * plan.groups + peer
                if kind == "down":
                    part = src.at[pl.ds(pl.multiple_of(at * (tall * PARTS), 16), tall * PARTS), lanes]
                else:
                    part = src.at[:, pl.ds(pl.multiple_of(at * tall, 16), tall), lanes]
                pltpu.make_async_copy(part, out.at[j, k], sem).start()


def attend_forward(plan, layer, ids, lens, x_ref, small, cosv, sinv, *refs):
    n = 7
    own, others, whole = weight_refs(plan, "attend", refs[: plan_inputs(plan, "attend")])
    refs = refs[plan_inputs(plan, "attend") :]
    normed, qkv, probs, mixed, resid, w, same, sem = refs
    width, tok = plan.width, plan.tok
    start_weights(plan, layer, "attend", ids, own, others, whole, w, sem)
    x = x_ref[...].astype(jnp.float32)
    hat, _ = normalize(x)
    low = (hat * small[0:1, :] + small[1:2, :]).astype(jnp.bfloat16)
    normed[...] = low
    first_end = lens[0]
    second_end = lens[0] + lens[1]

    def seg(axis):
        at = lax.broadcasted_iota(jnp.int32, (tok, tok), axis)
        return (at >= first_end).astype(jnp.int32) + (at >= second_end).astype(jnp.int32)

    same[...] = (seg(0) == seg(1)).astype(jnp.float32)
    wait_all(w, sem)
    for j in range(3):
        full = mm(low, w[j], 1, 0)
        if j == 2:
            qkv[:, j * width : (j + 1) * width] = full.astype(jnp.bfloat16)
            continue
        for t in range(width // LANES):
            part = full[:, t * LANES : (t + 1) * LANES]
            part = part * cosv[...] + swap_halves(part) * sinv[...]
            qkv[:, j * width + t * LANES : j * width + (t + 1) * LANES] = part.astype(jnp.bfloat16)

    def tile(t, carry):
        at = pl.multiple_of(t * LANES, LANES)
        q = qkv[:, pl.ds(at, LANES)]
        k = qkv[:, pl.ds(width + at, LANES)]
        v = qkv[:, pl.ds(2 * width + at, LANES)]
        total = None
        for h in range(2):
            scores = mm(head_of(q, h), k, 1, 1) * HEAD_DIM ** (-0.5)
            scores = jnp.where(same[...] > 0.5, scores, masked_score)
            peak = jnp.max(scores, axis=-1, keepdims=True)
            expd = jnp.exp(scores - peak)
            p = expd * (1.0 / jnp.sum(expd, axis=-1, keepdims=True))
            probs[2 * t + h] = p
            part = mm(p.astype(jnp.bfloat16), head_of(v, h), 1, 0)
            total = part if total is None else total + part
        mixed[:, pl.ds(at, LANES)] = total.astype(jnp.bfloat16)
        return carry

    lax.fori_loop(0, width // LANES, tile, 0)
    resid[...] = x + mm(mixed[...], w[3], 1, 0)


def feed_forward(plan, layer, ids, resid, small, *refs):
    a = plan_inputs(plan, "up")
    b = plan_inputs(plan, "down")
    up_refs = weight_refs(plan, "up", refs[:a])
    down_refs = weight_refs(plan, "down", refs[a : a + b])
    normed, active, slope, y, wu, wd, sem_u, sem_d = refs[a + b :]
    width = plan.width
    start_weights(plan, layer, "up", ids, *up_refs, wu, sem_u)
    start_weights(plan, layer, "down", ids, *down_refs, wd, sem_d)
    hat, _ = normalize(resid[...])
    low = (hat * small[2:3, :] + small[3:4, :]).astype(jnp.bfloat16)
    normed[...] = low
    wait_all(wu, sem_u)
    total = resid[...]
    for j in range(PARTS):
        v = mm(low, wu[j], 1, 0)
        cdf = 0.5 * (1.0 + lax.erf(v * (2.0**-0.5)))
        act = (v * cdf).astype(jnp.bfloat16)
        lanes = slice(j * width, (j + 1) * width)
        active[:, lanes] = act
        slope[:, lanes] = cdf + v * (jnp.exp(v * v * -0.5) * 0.3989422804014327)
        if j == 0:
            wait_all(wd, sem_d)
        total = total + mm(act, wd[lanes, :], 1, 0)
    y[...] = total.astype(jnp.bfloat16)


def down_grad(plan, ids, active, d_out, keep, send, g, sem):
    width = plan.width
    d = d_out[...]
    for j in range(PARTS):
        g[j * width : (j + 1) * width, :] = mm(
            active[:, j * width : (j + 1) * width], d, 0, 0
        ).astype(jnp.bfloat16)
    start_grads(plan, "down", ids, g, keep, send, sem)
    wait_all(g, sem)


def feed_backward(plan, layer, ids, d_out, resid, normed, slope, small, *refs):
    a = plan_inputs(plan, "up")
    b = plan_inputs(plan, "down")
    up_refs = weight_refs(plan, "up", refs[:a])
    down_refs = weight_refs(plan, "down", refs[a : a + b])
    keep, send, d_resid, sums, wu, wd, g, sem_u, sem_d, sem_g = refs[a + b :]
    width = plan.width
    start_weights(plan, layer, "down", ids, *down_refs, wd, sem_d)
    start_weights(plan, layer, "up", ids, *up_refs, wu, sem_u)
    d = d_out[...]
    low = normed[...]
    wait_all(wd, sem_d)
    total = None
    for j in range(PARTS):
        lanes = slice(j * width, (j + 1) * width)
        d_up = (mm(d, wd[lanes, :], 1, 1) * slope[:, lanes]).astype(jnp.bfloat16)
        g[j] = mm(low, d_up, 0, 0).astype(jnp.bfloat16)
        if j == 0:
            wait_all(wu, sem_u)
        part = mm(d_up, wu[j], 1, 1)
        total = part if total is None else total + part
    start_grads(plan, "up", ids, g, keep, send, sem_g)
    hat, scale = normalize(resid[...])
    sums[0:1, :] = jnp.sum(total * hat, axis=0, keepdims=True)
    sums[1:2, :] = jnp.sum(total, axis=0, keepdims=True)
    d_resid[...] = d.astype(jnp.float32) + norm_backward(total, hat, scale, small[2:3, :])
    wait_all(g, sem_g)


def attend_backward(plan, layer, ids, x_ref, d_resid, normed, qkv, probs, mixed, small, cosv, sinv, *refs):
    a = plan_inputs(plan, "attend")
    own, others, whole = weight_refs(plan, "attend", refs[:a])
    keep, send, dx, sums, w, g, d_mixed, d_qkv, sem_w, sem_g = refs[a:]
    width = plan.width
    start_weights(plan, layer, "attend", ids, own, others, whole, w, sem_w)
    d = d_resid[...].astype(jnp.bfloat16)
    g[3] = mm(mixed[...], d, 0, 0).astype(jnp.bfloat16)
    wait_all(w, sem_w)
    d_mixed[...] = mm(d, w[3], 1, 1).astype(jnp.bfloat16)

    def tile(t, carry):
        at = pl.multiple_of(t * LANES, LANES)
        q = qkv[:, pl.ds(at, LANES)]
        k = qkv[:, pl.ds(width + at, LANES)]
        v = qkv[:, pl.ds(2 * width + at, LANES)]
        dm = d_mixed[:, pl.ds(at, LANES)]
        dq = dk = dv = None
        for h in range(2):
            p = probs[2 * t + h]
            dm_h = head_of(dm, h)
            dv_h = mm(p.astype(jnp.bfloat16), dm_h, 0, 0)
            dp = mm(dm_h, v, 1, 1)
            ds = p * (dp - jnp.sum(dp * p, axis=-1, keepdims=True))
            ds = ds.astype(jnp.bfloat16)
            dq_h = mm(ds, head_of(k, h), 1, 0)
            dk_h = mm(ds, head_of(q, h), 0, 0)
            dq = dq_h if dq is None else dq + dq_h
            dk = dk_h if dk is None else dk + dk_h
            dv = dv_h if dv is None else dv + dv_h
        scale = HEAD_DIM ** (-0.5)
        dq = dq * scale
        dk = dk * scale
        dq = dq * cosv[...] - swap_halves(dq) * sinv[...]
        dk = dk * cosv[...] - swap_halves(dk) * sinv[...]
        d_qkv[:, pl.ds(at, LANES)] = dq.astype(jnp.bfloat16)
        d_qkv[:, pl.ds(width + at, LANES)] = dk.astype(jnp.bfloat16)
        d_qkv[:, pl.ds(2 * width + at, LANES)] = dv.astype(jnp.bfloat16)
        return carry

    lax.fori_loop(0, width // LANES, tile, 0)
    low = normed[...]
    total = None
    for j in range(3):
        part_in = d_qkv[:, j * width : (j + 1) * width]
        g[j] = mm(low, part_in, 0, 0).astype(jnp.bfloat16)
        part = mm(part_in, w[j], 1, 1)
        total = part if total is None else total + part
    start_grads(plan, "attend", ids, g, keep, send, sem_g)
    hat, scale = normalize(x_ref[...].astype(jnp.float32))
    sums[0:1, :] = jnp.sum(total * hat, axis=0, keepdims=True)
    sums[1:2, :] = jnp.sum(total, axis=0, keepdims=True)
    back = d_resid[...] + norm_backward(total, hat, scale, small[0:1, :])
    dx[...] = back.astype(jnp.bfloat16)
    wait_all(g, sem_g)


def pack(plan, ids, qkv, out, up, down, keep, send):
    width, tall = plan.width, plan.tall
    first = ids[0] == 0
    at = 0
    for ref in (qkv, out, up, down):
        for b in range(PARTS if ref is down else ref.shape[2] // width):
            if ref is down:
                block = ref[0, b * tall : (b + 1) * tall, :]
            else:
                block = ref[0, :, b * width : (b + 1) * width]
            low, high = block[:, :BLOCK], block[:, BLOCK:]
            keep[at] = jnp.where(first, low, high)
            send[at] = jnp.where(first, high, low)
            at += 1


def final_layout(plan, kind, ids, x, *outs):
    width, tall = plan.width, plan.tall
    core, group = ids[0], ids[1]
    tables = masks_of(plan.groups, False)
    for j in range(plan.groups):
        peer = group ^ pick(core == 0, tables[0][j], tables[1][j])
        for h in range(2):
            for b in range(PARTS):
                value = x[j, h ^ core, b].astype(jnp.float32)
                if kind == "down":
                    at = pl.multiple_of(peer * (tall * PARTS) + b * tall, 8)
                    outs[0][0, pl.ds(at, tall), h * BLOCK : (h + 1) * BLOCK] = value
                    continue
                at = pl.multiple_of(peer * tall, 8)
                out = outs[-1] if kind == "attend" and b == PARTS - 1 else outs[0]
                c = 0 if kind == "attend" and b == PARTS - 1 else b
                lanes = slice(c * width + h * BLOCK, c * width + (h + 1) * BLOCK)
                out[0, pl.ds(at, tall), lanes] = value


SHARDS = {"attend": 2, "up": 1, "down": 1}


def plan_inputs(plan, kind):
    return 2 * SHARDS[kind] + 4 if plan.direct else 1


def weight_refs(plan, kind, refs):
    if not plan.direct:
        return None, None, refs[0]
    n = SHARDS[kind]
    return (refs[:n], refs[n : 2 * n]), refs[2 * n :], None


DEPTH = 2
DEPTH_BACK = 3
SHIFT = 0
ROWS_FIRST = ()

VMEM = pl.BlockSpec(memory_space=pltpu.VMEM)
SMEM = pl.BlockSpec(memory_space=pltpu.SMEM)
HBM = pl.BlockSpec(memory_space=pl.ANY)


def call(body, name, args, specs, outs, out_specs, scratch, flops):
    moved = sum(x.size * x.dtype.itemsize for x in list(args) + list(outs))
    return pl.pallas_call(
        body,
        out_shape=outs,
        in_specs=specs,
        out_specs=out_specs,
        scratch_shapes=scratch,
        name=name,
        cost_estimate=pl.CostEstimate(flops=flops, transcendentals=0, bytes_accessed=moved),
        compiler_params=pltpu.CompilerParams(vmem_limit_bytes=58 << 20),
    )(*args)


def shape(dims, dtype):
    return jax.ShapeDtypeStruct(dims, dtype)


BF, F32 = jnp.bfloat16, jnp.float32


class Kernels:
    def __init__(self, plan, ids, lens, tables, heads):
        self.plan, self.ids, self.lens, self.tables, self.heads = plan, ids, lens, tables, heads
        self.part = pltpu.VMEM((PARTS, plan.width, plan.width), BF)
        self.tall = pltpu.VMEM((PARTS * plan.width, plan.width), BF)
        self.sem = pltpu.SemaphoreType.DMA(())

    def attend_forward(self, layer, x, small, weights):
        p = self.plan
        t, d = p.tok, p.width
        return call(
            functools.partial(attend_forward, p, layer),
            f"attend_forward_{layer}",
            (self.ids, self.lens, x, small, *self.tables, *weights),
            [SMEM, SMEM] + [VMEM] * 4 + [HBM] * len(weights),
            (
                shape((t, d), BF),
                shape((t, 3 * d), BF),
                shape((self.heads, t, t), F32),
                shape((t, d), BF),
                shape((t, d), F32),
            ),
            (VMEM,) * 5,
            [self.part, pltpu.VMEM((t, t), F32), self.sem],
            2 * t * d * d * 4 + 4 * self.heads * t * t * LANES,
        )

    def feed_forward(self, layer, resid, small, weights):
        p = self.plan
        t, d = p.tok, p.width
        return call(
            functools.partial(feed_forward, p, layer),
            f"feed_forward_{layer}",
            (self.ids, resid, small, *weights),
            [SMEM, VMEM, VMEM] + [HBM] * len(weights),
            (
                shape((t, d), BF),
                shape((t, PARTS * d), BF),
                shape((t, PARTS * d), F32),
                shape((t, d), BF),
            ),
            (VMEM,) * 4,
            [self.part, self.tall, self.sem, self.sem],
            2 * t * d * d * 8,
        )

    def grads(self, kind):
        p = self.plan
        rows = p.tall * PARTS if kind == "down" else None
        if not p.direct:
            dims = (PARTS * p.width, BLOCK) if kind == "down" else (PARTS, p.width, BLOCK)
        elif kind == "down":
            dims = (p.groups, p.rows, rows, BLOCK)
        else:
            dims = (p.groups, p.rows, PARTS, p.tall, BLOCK)
        return (shape(dims, BF), shape(dims, BF))

    def down_grad(self, layer, active, d_out):
        p = self.plan
        return call(
            functools.partial(down_grad, p),
            f"down_grad_{layer}",
            (self.ids, active, d_out),
            [SMEM, VMEM, VMEM],
            self.grads("down"),
            (HBM, HBM),
            [self.tall, self.sem],
            2 * p.tok * p.width * p.width * 4,
        )

    def feed_backward(self, layer, d_out, resid, normed, slope, small, weights):
        p = self.plan
        t, d = p.tok, p.width
        return call(
            functools.partial(feed_backward, p, layer),
            f"feed_backward_{layer}",
            (self.ids, d_out, resid, normed, slope, small, *weights),
            [SMEM] + [VMEM] * 5 + [HBM] * len(weights),
            (*self.grads("up"), shape((t, d), F32), shape((2, d), F32)),
            (HBM, HBM, VMEM, VMEM),
            [self.part, self.tall, self.part, self.sem, self.sem, self.sem],
            2 * t * d * d * 12,
        )

    def attend_backward(self, layer, x, d_resid, normed, qkv, probs, mixed, small, weights):
        p = self.plan
        t, d = p.tok, p.width
        return call(
            functools.partial(attend_backward, p, layer),
            f"attend_backward_{layer}",
            (self.ids, x, d_resid, normed, qkv, probs, mixed, small, *self.tables, *weights),
            [SMEM] + [VMEM] * 9 + [HBM] * len(weights),
            (*self.grads("attend"), shape((t, d), BF), shape((2, d), F32)),
            (HBM, HBM, VMEM, VMEM),
            [self.part, self.part, pltpu.VMEM((t, d), BF), pltpu.VMEM((t, 3 * d), BF), self.sem, self.sem],
            2 * t * d * d * 8 + 10 * self.heads * t * t * LANES,
        )


    def pack(self, shards):
        p = self.plan
        dims = (3 * PARTS, p.tall, BLOCK)
        specs = []
        for i, w in enumerate(shards):
            tall = p.tall * PARTS if i == len(shards) - 1 else p.tall
            specs.append(pl.BlockSpec((1, tall, w.shape[2]), lambda i, ids: (0, ids[1], 0)))
        whole = pl.BlockSpec(dims, lambda i, ids: (0, 0, 0))
        return pl.pallas_call(
            functools.partial(pack, p),
            out_shape=(shape(dims, BF),) * 2,
            grid_spec=pltpu.PrefetchScalarGridSpec(
                num_scalar_prefetch=1, grid=(1,), in_specs=specs, out_specs=(whole, whole)
            ),
            name="pack",
        )(self.ids, *shards)

    def final(self, kind, x):
        p = self.plan
        share, d = p.width // p.rows, p.width
        dims = {"attend": ((share, 3 * d), (share, d)), "up": ((share, PARTS * d),), "down": ((share * PARTS, d),)}
        outs = tuple(shape((1, *dim), F32) for dim in dims[kind])
        return call(
            functools.partial(final_layout, p, kind),
            f"final_{kind}",
            (self.ids, x),
            [SMEM, VMEM],
            outs,
            (VMEM,) * len(outs),
            [],
            0,
        )


def swap_cores(x):
    return lax.ppermute(x, "section", [(0, 1), (1, 0)])


def stage_bits(groups):
    bits = [1 << i for i in range(groups.bit_length() - 1)]
    turn = len(bits) // 2
    return bits, bits[turn:] + bits[:turn]


def swap_groups(x, groups, stage):
    pairs = []
    for core, bits in enumerate(stage_bits(groups)):
        pairs += [(core * groups + g, core * groups + (g ^ bits[stage])) for g in range(groups)]
    return lax.ppermute(x, ("section", "group"), pairs)


def along(x, distance):
    rows = lax.axis_size("dp")
    return lax.ppermute(x, "dp", [(i, (i + distance) % rows) for i in range(rows)])


def gate(x, after):
    return lax.optimization_barrier((x, *after))[0] if after else x


def swap_rows(x, bit):
    rows = lax.axis_size("dp")
    return lax.ppermute(x, "dp", [(i, i ^ bit) for i in range(rows)])


KINDS = ("attend", "up", "down")


def piece_of(plan, group, kind, shards):
    tall = plan.tall

    def cut(w, inside):
        if inside:
            w = lax.dynamic_slice_in_dim(w[0], group * (tall * PARTS), tall * PARTS, 0)
            return w.reshape(PARTS, tall, 2, BLOCK).transpose(2, 0, 1, 3)
        w = lax.dynamic_slice_in_dim(w[0], group * tall, tall, 0)
        return w.reshape(tall, -1, 2, BLOCK).transpose(2, 1, 0, 3)

    return jnp.concatenate([cut(w, kind == "down") for w in shards], axis=1)


def whole_of(plan, core, group, row, kind, shard, half_mine, half_theirs):
    groups, rows, tall = plan.groups, plan.rows, plan.tall
    tables = jnp.array(masks_of(groups, True), jnp.int32)
    first = core == 0
    halves = []
    for h in range(2):
        got = jnp.where(core == h, half_mine, half_theirs)
        got = jnp.take(got, jnp.argsort(group ^ tables[h]), axis=0)
        own = []
        for w in shard:
            if kind == "down":
                w = w[0].reshape(groups, PARTS, tall, 2, BLOCK)[:, :, :, h]
            else:
                w = w[0].reshape(groups, tall, -1, 2, BLOCK)[:, :, :, h].transpose(0, 2, 1, 3)
            own.append(w)
        own = jnp.concatenate(own, axis=1)[:, None]
        got = jnp.concatenate([got, own], axis=1)
        held = jnp.stack([row_from(plan, row, k) for k in range(rows - 1)] + [row])
        got = jnp.take(got, jnp.argsort(held), axis=1)
        if kind == "down":
            halves.append(got.transpose(1, 0, 2, 3, 4).reshape(PARTS * plan.width, BLOCK))
        else:
            halves.append(got.transpose(2, 1, 0, 3, 4).reshape(PARTS, plan.width, BLOCK))
    return jnp.stack(halves)


def ordered_grads(plan, kind, core, group, row, keep, send):
    groups, rows, tall = plan.groups, plan.rows, plan.tall
    tables = jnp.array(masks_of(groups, False), jnp.int32)
    outs = []
    for x, half in ((keep, core), (send, 1 - core)):
        if kind == "down":
            x = x.reshape(rows, groups, PARTS, tall, BLOCK).transpose(1, 0, 2, 3, 4)
        else:
            x = x.reshape(PARTS, rows, groups, tall, BLOCK).transpose(2, 1, 0, 3, 4)
        x = jnp.take(x, group ^ jnp.where(half == 0, tables[0], tables[1]), axis=0)
        x = jnp.take(x, jnp.stack([row_to(plan, row, k) for k in range(rows)]), axis=1)
        outs.append(x)
    return outs


def on_device(
    tokens,
    cotangent,
    lengths,
    attend_gain,
    attend_bias,
    qkv_weight,
    out_weight,
    feed_gain,
    feed_bias,
    up_weight,
    down_weight,
):
    core = lax.axis_index("section")
    group = lax.axis_index("group")
    row = lax.axis_index("dp")
    groups = lax.axis_size("group")
    rows = lax.axis_size("dp")
    stages = groups.bit_length() - 1
    tok, width = tokens.shape[1:]
    plan = Plan(groups, rows, tok, width)
    few = plan.few
    first = core == 0
    share = width // rows
    ids = jnp.stack([core, group, row]).astype(jnp.int32)
    lens = lax.dynamic_index_in_dim(lengths, core, 0, False)[0]

    shards = {"attend": (qkv_weight, out_weight), "up": (up_weight,), "down": (down_weight,)}
    chunks = [(layer, kind) for layer in range(2) for kind in KINDS]
    n_chunks = len(chunks)
    x0 = lax.dynamic_index_in_dim(tokens, core, 0, False)
    cot = lax.dynamic_index_in_dim(cotangent, core, 0, False)
    cosine, sine, _ = rope_tables(lens, tok)
    kernels = Kernels(plan, ids, lens, (cosine, sine), width // HEAD_DIM)
    history = {}
    pieces, bufs, gots, theirs, saved = {}, {}, {}, {}, {}
    xs = {0: x0}
    small = jnp.stack([attend_gain[0], attend_bias[0], feed_gain[0], feed_bias[0]])[None]

    if plan.direct:
        keep, send = kernels.pack([w for kind in KINDS for w in shards[kind]])
    else:
        both = jnp.concatenate([piece_of(plan, group, kind, shards[kind]) for kind in KINDS], axis=1)
        keep = lax.dynamic_index_in_dim(both, core, 0, False)
        send = lax.dynamic_index_in_dim(both, 1 - core, 0, False)
    got = swap_cores(send)
    for layer in range(2):
        part = jnp.where(core == layer, keep, got)
        for i, kind in enumerate(KINDS):
            pieces[layer, kind] = part[i * PARTS : (i + 1) * PARTS][None, None]

    def weights_of(layer, kind):
        parts = [*bufs[layer, kind], *gots[layer, kind]]
        if plan.direct:
            if kind == "down":
                parts = [p.reshape(*p.shape[:2], PARTS * plan.tall, BLOCK) for p in parts]
            return (*shards[kind], *theirs[kind], *parts)
        mine, other = (jnp.concatenate(p, axis=0) for p in (parts[:2], parts[2:]))
        shard = [jnp.where(core == layer, a, b) for a, b in zip(shards[kind], theirs[kind])]
        return (whole_of(plan, core, group, row, kind, shard, mine, other),)

    def run_attend(layer, after):
        x = gate(xs[layer], after)
        out = kernels.attend_forward(layer, x, smalls[layer], weights_of(layer, "attend"))
        saved[layer, "attend"] = out
        return out[4]

    def run_feed(layer, after):
        resid = gate(saved[layer, "attend"][4], after)
        weights = weights_of(layer, "up") + weights_of(layer, "down")
        *out, y = kernels.feed_forward(layer, resid, smalls[layer], weights)
        saved[layer, "feed"] = out
        xs[layer + 1] = y
        return y

    row_bits = [1 << i for i in range(rows.bit_length() - 1)]
    hops = len(row_bits) if few else 1
    depth = hops + stages
    kernel_at = {depth + SHIFT: (run_attend, 0), depth + 2 + SHIFT: (run_feed, 0), depth + 3 + SHIFT: (run_attend, 1)}
    small_steps = row_bits + [0]
    gotten = {}
    for slot in range(n_chunks + depth + 1):
        after = history.get(slot - DEPTH, [])
        done = []
        for stage in range(depth, -1, -1):
            c = slot - stage
            if not 0 <= c < n_chunks:
                continue
            chunk = chunks[c]
            if stage == depth:
                gots[chunk].append(swap_cores(gate(bufs[chunk][1], after)))
                done.append(gots[chunk][-1])
                continue
            if stage < hops:
                piece = pieces[chunk]
                if few:
                    got = swap_rows(gate(piece, after), row_bits[hops - 1 - stage])
                    pieces[chunk] = jnp.concatenate([piece, got], axis=1)
                    gotten.setdefault(chunk, []).append(got)
                else:
                    got = lax.all_gather(gate(piece[0, 0], after), "dp")
                    back = (row - 1 - jnp.arange(rows - 1)) % rows
                    gotten[chunk] = [jnp.take(got, back, axis=0)[None]]
                done.append(got)
                continue
            if stage == hops:
                bufs[chunk] = jnp.concatenate(gotten[chunk], axis=1)
            buf = bufs[chunk]
            got = swap_groups(gate(buf, after), groups, stage - hops)
            done.append(got)
            if stage + 1 < depth:
                bufs[chunk] = jnp.concatenate([buf, got], axis=0)
            else:
                bufs[chunk] = [buf, got]
                gots[chunk] = [swap_cores(gate(buf, after))]
                done.append(gots[chunk][0])
        if few and slot < len(small_steps):
            bit = small_steps[slot]
            held = gate(small, history.get(slot - 1, []))
            got = swap_rows(held, bit) if bit else swap_cores(held)
            done.append(got)
            small = jnp.concatenate([small, got])
        elif slot == 0:
            small = lax.all_gather(small, ("section", "dp"))
        if slot == (len(small_steps) if few else 1):
            got = small.reshape(2, rows, PARTS, share)
            if few:
                got = jnp.take(got, row ^ jnp.arange(rows), axis=1)
                got = jnp.take(got, core ^ jnp.arange(2), axis=0)
            smalls = got.transpose(0, 2, 1, 3).reshape(2, PARTS, width).astype(F32)
        if 1 <= slot <= len(KINDS):
            kind = KINDS[slot - 1]
            theirs[kind] = tuple(swap_cores(gate(w, history[slot - 1])) for w in shards[kind])
            done += theirs[kind]
        if slot in kernel_at:
            run, layer = kernel_at[slot]
            done.append(run(layer, history[slot - 1]))
        history[slot] = done
    run_feed(1, [])

    grads, backs, sums = {}, [None, None], {}
    order = [(layer, kind) for layer in (1, 0) for kind in ("down", "up", "attend")]

    def run_backward(flow, layer, kind, after):
        normed, qkv, probs, mixed, resid = saved[layer, "attend"]
        normed_two, active, slope = saved[layer, "feed"]
        d_out, d_resid = flow
        if kind == "down":
            return kernels.down_grad(layer, active, gate(d_out, after)), flow
        if kind == "up":
            weights = weights_of(layer, "up") + weights_of(layer, "down")
            *g, d_resid, sums[layer, kind] = kernels.feed_backward(
                layer, gate(d_out, after), resid, normed_two, slope, smalls[layer], weights
            )
            return g, (d_out, d_resid)
        *g, d_x, sums[layer, kind] = kernels.attend_backward(
            layer,
            xs[layer],
            gate(d_resid, after),
            normed,
            qkv,
            probs,
            mixed,
            smalls[layer],
            weights_of(layer, "attend"),
        )
        backs[layer] = d_x
        return g, (d_x, d_resid)

    def total_of(parts):
        total = parts[0].astype(F32)
        for part in parts[1:]:
            total = total + part.astype(F32)
        return total.astype(BF)

    def ready(kind, keep, send):
        if plan.direct:
            dims = (groups, rows, PARTS, plan.tall, BLOCK)
            return {"sum": [keep.reshape(dims), send.reshape(dims)]}
        return {"sum": ordered_grads(plan, kind, core, group, row, keep, send)}

    def way_of(kind):
        over_groups = [(0, i) for i in range(stages)]
        over_rows = [(1, bit) for bit in row_bits] if few else [(1, 0)]
        return over_rows + over_groups if few and kind in ROWS_FIRST else over_groups + over_rows

    last = 1 + stages + hops

    def step(kind, parts, stage, after):
        if stage == 0:
            parts["sum"] = [parts["sum"][0], swap_cores(gate(parts["sum"][1], after))]
            parts["left"] = [groups, rows]
            return parts["sum"][1]
        axis, bit = way_of(kind)[stage - 1]
        if axis == 1 and not few:
            send = total_of([p[0] for p in parts["sum"]])
            held = jnp.argsort(jnp.stack([row_to(plan, row, k) for k in range(rows)]))
            send = gate(jnp.take(send, held, axis=0), after)
            got = lax.psum_scatter(send, "dp", scatter_dimension=0, tiled=True)
            parts["sum"] = [got[None]]
            parts["left"] = [1, 1]
            return got
        low, high = [0, 0], list(parts["left"])
        low[axis] = high[axis] // 2
        send = total_of([p[low[0] : high[0], low[1] : high[1]] for p in parts["sum"]])
        parts["left"][axis] //= 2
        send = gate(send, after)
        got = swap_groups(send, groups, bit) if axis == 0 else swap_rows(send, bit)
        parts["sum"] = parts["sum"] + [got]
        return got

    def result_of(parts):
        return total_of([p[:1, 0] for p in parts["sum"]])

    history = {}
    flow = (cot, None)
    g, flow = run_backward(flow, *order[0], [])
    live = {0: ready(order[0][1], *g)}
    final = {}
    small_sum, small_stage = None, 0
    for slot in range(n_chunks + last + stages + 1):
        after = history.get(slot - DEPTH_BACK, [])
        done = []
        for c in range(n_chunks):
            if 0 <= slot - c < last:
                done.append(step(order[c][1], live[c], slot - c, after))
        for i, kind in enumerate(("down", "up", "attend")):
            stage = slot - (i + len(KINDS) + last)
            if stage == 0:
                low, high = (result_of(live[order.index((layer, kind))]) for layer in range(2))
                other = swap_cores(jnp.where(first, high, low))
                final[kind] = jnp.stack([jnp.where(first, low, high), other], axis=1)
                done.append(other)
            elif 1 <= stage <= stages:
                got = swap_groups(gate(final[kind], after), groups, stages - stage)
                final[kind] = jnp.concatenate([final[kind], got], axis=0)
                done.append(got)
        if slot + 1 < n_chunks:
            layer, kind = order[slot + 1]
            g, flow = run_backward(flow, layer, kind, history.get(slot - 1, []))
            live[slot + 1] = ready(kind, *g)
            done.append(flow[0] if kind == "attend" else flow[1] if kind == "up" else g[0])
        if slot + 1 == n_chunks:
            small_sum = jnp.stack([jnp.concatenate([sums[i, "attend"], sums[i, "up"]]) for i in range(2)])
        if small_sum is not None and small_stage <= stages + len(row_bits):
            held = gate(small_sum, history.get(slot - 1, []))
            if small_stage == 0:
                got = swap_cores(held)
            elif small_stage <= stages:
                got = swap_groups(held, groups, small_stage - 1)
            else:
                got = swap_rows(held, row_bits[small_stage - stages - 1])
            small_stage += 1
            small_sum = small_sum + got
        history[slot] = done

    def home(low, high):
        got = swap_cores(jnp.where(first, high, low))
        keep = jnp.where(first, low, high)
        return jnp.where(first, jnp.stack([keep, got]), jnp.stack([got, keep]))

    layer_out = home(xs[1], xs[2])
    input_grad = home(*backs)

    def outside(x):
        return x.transpose(0, 3, 2, 1, 4).reshape(1, share, -1).astype(F32)

    if plan.direct:
        qkv_grad, out_grad = kernels.final("attend", final["attend"])
        (up_grad,) = kernels.final("up", final["up"])
        (down_grads,) = kernels.final("down", final["down"])
    else:
        tables = jnp.array(masks_of(groups, False), jnp.int32)
        at = jnp.argsort(group ^ jnp.where(first, tables[0], tables[1]))
        for kind in KINDS:
            x = jnp.take(final[kind], at, axis=0)
            final[kind] = jnp.take(x, jnp.arange(2) ^ core, axis=1)
        qkv_grad = outside(final["attend"][:, :, 0:3])
        out_grad = outside(final["attend"][:, :, 3:4])
        up_grad = outside(final["up"])
        down_grads = final["down"].transpose(0, 2, 3, 1, 4).reshape(1, -1, width).astype(F32)

    small_grads = small_sum
    own = lax.dynamic_index_in_dim(small_grads, core, 0, False)
    own = lax.dynamic_slice_in_dim(own, row * share, share, 1)
    return (
        layer_out[None],
        input_grad[None],
        own[0][None],
        own[1][None],
        qkv_grad,
        out_grad,
        own[2][None],
        own[3][None],
        up_grad,
        down_grads,
    )


def solution(mesh):
    placed = (
        P(None, ("group", "dp"), None),
        P(None, ("group", "dp"), None),
        P(None, ("group", "dp"), None),
        P("section", "dp"),
        P("section", "dp"),
        P("section", "dp", None),
        P("section", "dp", None),
        P("section", "dp"),
        P("section", "dp"),
        P("section", "dp", None),
        P("section", "dp", None),
    )
    return jax.shard_map(
        on_device,
        mesh=mesh,
        in_specs=placed,
        out_specs=(
            P("section", None, ("group", "dp"), None),
            P("section", None, ("group", "dp"), None),
            P("section", "dp"),
            P("section", "dp"),
            P("section", "dp", None),
            P("section", "dp", None),
            P("section", "dp"),
            P("section", "dp"),
            P("section", "dp", None),
            P("section", "dp", None),
        ),
        check_vma=False,
    )
```

```python
import functools

import jax
import jax.numpy as jnp
from jax import lax
from jax.experimental import pallas as pl
from jax.experimental.pallas import tpu as pltpu
from jax.sharding import PartitionSpec as P

HEAD_DIM = 64
LANES = 128
BLOCK = 384
PARTS = 4


masked_score = -1000000000.0


def rope_tables(lengths_row, tok):
    bounds = jnp.cumsum(lengths_row, dtype=jnp.int32)
    places = jnp.arange(tok, dtype=jnp.int32)
    segment = jnp.sum((places[:, None] >= bounds[None, :-1]).astype(jnp.int32), axis=1)
    starts = bounds - lengths_row
    picks = jnp.arange(lengths_row.shape[0], dtype=jnp.int32)
    begin = jnp.sum(jnp.where(segment[:, None] == picks[None, :], starts[None, :], 0), axis=1)
    offset = (places - begin).astype(jnp.float32)
    half = HEAD_DIM // 2
    freqs = 10000.0 ** (-jnp.arange(half, dtype=jnp.float32) / half)
    angles = offset[:, None] * freqs[None, :]
    cosine, sine = jnp.cos(angles), jnp.sin(angles)
    heads = LANES // HEAD_DIM
    cosine = jnp.concatenate([cosine, cosine] * heads, axis=1)
    sine = jnp.concatenate([-sine, sine] * heads, axis=1)
    return cosine, sine, segment


def mm(left, right, left_dim, right_dim):
    return lax.dot_general(
        left, right, (((left_dim,), (right_dim,)), ((), ())), preferred_element_type=jnp.float32
    )


def normalize(x):
    center = x - jnp.mean(x, axis=-1, keepdims=True)
    spread = jnp.mean(center * center, axis=-1, keepdims=True)
    scale = lax.rsqrt(spread + 1e-05)
    return center * scale, scale


def norm_backward(d_out, hat, scale, gain):
    d_hat = d_out * gain
    part = d_hat - jnp.mean(d_hat, axis=-1, keepdims=True)
    part = part - hat * jnp.mean(d_hat * hat, axis=-1, keepdims=True)
    return part * scale


def swap_halves(x):
    half = HEAD_DIM // 2
    lane = lax.broadcasted_iota(jnp.int32, x.shape, 1)
    low = lane % HEAD_DIM < half
    return jnp.where(low, pltpu.roll(x, LANES - half, 1), pltpu.roll(x, half, 1))


def head_of(x, which):
    lane = lax.broadcasted_iota(jnp.int32, x.shape, 1)
    inside = lane < HEAD_DIM if which == 0 else lane >= HEAD_DIM
    return jnp.where(inside, x, jnp.zeros_like(x))


def masks_of(groups, low_first):
    bits = [1 << i for i in range(groups.bit_length() - 1)]
    turn = len(bits) // 2
    tables = []
    for order in (bits, bits[turn:] + bits[:turn]):
        if not low_first:
            order = order[::-1]
        tables.append([sum(b for t, b in enumerate(order) if (j >> t) & 1) for j in range(groups)])
    return tables


def row_masks(rows):
    bits = [1 << i for i in reversed(range(rows.bit_length() - 1))]
    return [sum(b for t, b in enumerate(bits) if (k >> t) & 1) for k in range(rows)]


def row_to(plan, row, k):
    return row ^ row_masks(plan.rows)[k] if plan.few else (row + k) % plan.rows


def row_from(plan, row, k):
    if plan.few:
        return row ^ row_masks(plan.rows)[k + 1]
    return (row + (plan.rows - 1 - k)) % plan.rows


def pick(flag, a, b):
    return a if a == b else jnp.where(flag, a, b)


class Plan:
    def __init__(self, groups, rows, tok, width):
        self.groups = groups
        self.rows = rows
        self.tok = tok
        self.width = width
        self.pieces = groups * rows
        self.tall = width // self.pieces
        self.direct = self.tall % 16 == 0
        self.few = rows <= 4 and rows & (rows - 1) == 0

    def rows_first(self, layer, kind):
        return self.few and self.direct and (layer, kind) in ROWS_FIRST


def start_weights(plan, layer, kind, ids, own, others, whole, dst, sem):
    width, tall = plan.width, plan.tall
    if not plan.direct:
        for h in range(2):
            lanes = pl.ds(h * BLOCK, BLOCK)
            if kind == "down":
                pltpu.make_async_copy(whole.at[h], dst.at[:, lanes], sem).start()
            else:
                pltpu.make_async_copy(whole.at[h], dst.at[:, :, lanes], sem).start()
        return
    core, group, row = ids[0], ids[1], ids[2]
    share = width // plan.rows
    mine, theirs = own

    def from_shard(refs):
        if kind == "down":
            at = pl.multiple_of(row * (share * PARTS), 16)
            pltpu.make_async_copy(refs[0].at[0], dst.at[pl.ds(at, share * PARTS)], sem).start()
            return
        at = pl.multiple_of(row * share, 16)
        j = 0
        for ref in refs:
            for b in range(ref.shape[2] // width):
                pltpu.make_async_copy(
                    ref.at[0, :, pl.ds(b * width, width)], dst.at[j, pl.ds(at, share)], sem
                ).start()
                j += 1

    @pl.when(core == layer)
    def _():
        from_shard(mine)

    @pl.when(core != layer)
    def _():
        from_shard(theirs)

    tables = masks_of(plan.groups, True)
    for half, flag, sources in ((core, core == 0, others[:2]), (1 - core, core != 0, others[2:])):
        lanes = pl.ds(pl.multiple_of(half * BLOCK, LANES), BLOCK)
        for j in range(plan.groups):
            peer = group ^ pick(flag, tables[0][j], tables[1][j])
            source = sources[j // (plan.groups // 2)]
            for k in range(plan.rows - 1):
                at = row_from(plan, row, k) * plan.groups + peer
                if kind == "down":
                    at = pl.multiple_of(at * (tall * PARTS), 16)
                    to = dst.at[pl.ds(at, tall * PARTS), lanes]
                else:
                    to = dst.at[:, pl.ds(pl.multiple_of(at * tall, 16), tall), lanes]
                pltpu.make_async_copy(source.at[j % (plan.groups // 2), k], to, sem).start()


def wait_all(ref, sem):
    pltpu.make_async_copy(ref, ref, sem).wait()


def start_grads(plan, kind, ids, src, outs, sem, rows_first):
    tall = plan.tall
    core, group, row = ids[0], ids[1], ids[2]
    if not plan.direct:
        pltpu.make_async_copy(src, outs[0], sem).start()
        return
    tables = masks_of(plan.groups, False)
    half = plan.groups // 2
    for j in range(plan.groups):
        peer = group ^ pick(core == 0, tables[0][j], tables[1][j])
        for k in range(plan.rows):
            at = row_to(plan, row, k) * plan.groups + peer
            if kind == "down":
                part = src.at[pl.ds(pl.multiple_of(at * (tall * PARTS), 16), tall * PARTS)]
            else:
                part = src.at[:, pl.ds(pl.multiple_of(at * tall, 16), tall)]
            if rows_first:
                out = outs[k // (plan.rows // 2)].at[j, k % (plan.rows // 2)]
            else:
                out = outs[j // half].at[j % half, k]
            pltpu.make_async_copy(part, out, sem).start()


def attend_forward(plan, layer, ids, lens, x_ref, small, cosv, sinv, *refs):
    n = 7
    own, others, whole = weight_refs(plan, "attend", refs[: plan_inputs(plan, "attend")])
    refs = refs[plan_inputs(plan, "attend") :]
    qkv, probs, acts, resid, w, same, sem = refs
    width, tok = plan.width, plan.tok
    start_weights(plan, layer, "attend", ids, own, others, whole, w, sem)
    x = x_ref[...].astype(jnp.float32)
    hat, _ = normalize(x)
    low = (hat * small[0:1, :] + small[1:2, :]).astype(jnp.bfloat16)
    acts[:, :width] = low
    first_end = lens[0]
    second_end = lens[0] + lens[1]

    def seg(axis):
        at = lax.broadcasted_iota(jnp.int32, (tok, tok), axis)
        return (at >= first_end).astype(jnp.int32) + (at >= second_end).astype(jnp.int32)

    same[...] = (seg(0) == seg(1)).astype(jnp.float32)
    wait_all(w, sem)
    for j in range(3):
        full = mm(low, w[j], 1, 0)
        if j == 2:
            qkv[:, j * width : (j + 1) * width] = full.astype(jnp.bfloat16)
            continue
        for t in range(width // LANES):
            part = full[:, t * LANES : (t + 1) * LANES]
            part = part * cosv[...] + swap_halves(part) * sinv[...]
            qkv[:, j * width + t * LANES : j * width + (t + 1) * LANES] = part.astype(jnp.bfloat16)

    def tile(t, carry):
        at = pl.multiple_of(t * LANES, LANES)
        q = qkv[:, pl.ds(at, LANES)]
        k = qkv[:, pl.ds(width + at, LANES)]
        v = qkv[:, pl.ds(2 * width + at, LANES)]
        total = None
        for h in range(2):
            scores = mm(head_of(q, h), k, 1, 1) * HEAD_DIM ** (-0.5)
            scores = jnp.where(same[...] > 0.5, scores, masked_score)
            peak = jnp.max(scores, axis=-1, keepdims=True)
            expd = jnp.exp(scores - peak)
            p = expd * (1.0 / jnp.sum(expd, axis=-1, keepdims=True))
            probs[2 * t + h] = p
            part = mm(p.astype(jnp.bfloat16), head_of(v, h), 1, 0)
            total = part if total is None else total + part
        acts[:, pl.ds(width + at, LANES)] = total.astype(jnp.bfloat16)
        return carry

    lax.fori_loop(0, width // LANES, tile, 0)
    resid[...] = x + mm(acts[:, width:], w[3], 1, 0)


def feed_forward(plan, layer, ids, resid, small, *refs):
    a = plan_inputs(plan, "up")
    b = plan_inputs(plan, "down")
    up_refs = weight_refs(plan, "up", refs[:a])
    down_refs = weight_refs(plan, "down", refs[a : a + b])
    acts, slope, y, wu, wd, sem_u, sem_d = refs[a + b :]
    width = plan.width
    start_weights(plan, layer, "up", ids, *up_refs, wu, sem_u)
    start_weights(plan, layer, "down", ids, *down_refs, wd, sem_d)
    hat, _ = normalize(resid[...])
    low = (hat * small[2:3, :] + small[3:4, :]).astype(jnp.bfloat16)
    acts[:, PARTS * width :] = low
    wait_all(wu, sem_u)
    total = resid[...]
    for j in range(PARTS):
        v = mm(low, wu[j], 1, 0)
        cdf = 0.5 * (1.0 + lax.erf(v * (2.0**-0.5)))
        act = (v * cdf).astype(jnp.bfloat16)
        lanes = slice(j * width, (j + 1) * width)
        acts[:, lanes] = act
        slope[:, lanes] = cdf + v * (jnp.exp(v * v * -0.5) * 0.3989422804014327)
        if j == 0:
            wait_all(wd, sem_d)
        total = total + mm(act, wd[lanes, :], 1, 0)
    y[...] = total.astype(jnp.bfloat16)


def split(first, own, send, at, x):
    low, high = x[:, :BLOCK], x[:, BLOCK:]
    own[:, at : at + BLOCK] = jnp.where(first, low, high)
    send[:, at : at + BLOCK] = jnp.where(first, high, low)


def both(own, other, lanes):
    return jnp.concatenate([own[:, lanes], other[:, lanes]], axis=0)


def down_grad(plan, rows_first, at, ids, active, active_too, d, d_too, *refs):
    *outs, g, sem = refs
    width = plan.width
    right = both(d, d_too, slice(at, at + BLOCK))
    for j in range(PARTS):
        lanes = slice(j * width, (j + 1) * width)
        g[lanes, :] = mm(both(active, active_too, lanes), right, 0, 0).astype(jnp.bfloat16)
    start_grads(plan, "down", ids, g, outs, sem, rows_first)
    wait_all(g, sem)


def up_grad(plan, rows_first, ids, normed, normed_too, d, d_too, *refs):
    *outs, g, sem = refs
    left = both(normed, normed_too, slice(0, plan.width))
    for j in range(0, PARTS, 2):
        two = mm(left, both(d, d_too, slice(j * BLOCK, (j + 2) * BLOCK)), 0, 0).astype(jnp.bfloat16)
        g[j] = two[:, :BLOCK]
        g[j + 1] = two[:, BLOCK:]
    start_grads(plan, "up", ids, g, outs, sem, rows_first)
    wait_all(g, sem)


def attend_grad(plan, rows_first, ids, acts, acts_too, d, d_too, *refs):
    *outs, g, sem = refs
    width = plan.width
    left = both(acts, acts_too, slice(0, width))
    two = mm(left, both(d, d_too, slice(0, 2 * BLOCK)), 0, 0).astype(jnp.bfloat16)
    g[0] = two[:, :BLOCK]
    g[1] = two[:, BLOCK:]
    g[2] = mm(left, both(d, d_too, slice(2 * BLOCK, 3 * BLOCK)), 0, 0).astype(jnp.bfloat16)
    left = both(acts, acts_too, slice(width, 2 * width))
    g[3] = mm(left, both(d, d_too, slice(3 * BLOCK, 4 * BLOCK)), 0, 0).astype(jnp.bfloat16)
    start_grads(plan, "attend", ids, g, outs, sem, rows_first)
    wait_all(g, sem)


def feed_backward(plan, layer, ids, d_out, resid, slope, small, *refs):
    a = plan_inputs(plan, "up")
    b = plan_inputs(plan, "down")
    up_refs = weight_refs(plan, "up", refs[:a])
    down_refs = weight_refs(plan, "down", refs[a : a + b])
    own, send, d_resid, sums, wu, wd, sem_u, sem_d = refs[a + b :]
    width = plan.width
    start_weights(plan, layer, "down", ids, *down_refs, wd, sem_d)
    start_weights(plan, layer, "up", ids, *up_refs, wu, sem_u)
    d = d_out[...]
    wait_all(wd, sem_d)
    total = None
    for j in range(PARTS):
        lanes = slice(j * width, (j + 1) * width)
        d_up = (mm(d, wd[lanes, :], 1, 1) * slope[:, lanes]).astype(jnp.bfloat16)
        split(ids[0] == 0, own, send, j * BLOCK, d_up)
        if j == 0:
            wait_all(wu, sem_u)
        part = mm(d_up, wu[j], 1, 1)
        total = part if total is None else total + part
    hat, scale = normalize(resid[...])
    sums[0:1, :] = jnp.sum(total * hat, axis=0, keepdims=True)
    sums[1:2, :] = jnp.sum(total, axis=0, keepdims=True)
    d_resid[...] = d.astype(jnp.float32) + norm_backward(total, hat, scale, small[2:3, :])


def attend_backward(plan, layer, ids, x_ref, d_resid, qkv, probs, small, cosv, sinv, *refs):
    a = plan_inputs(plan, "attend")
    shard, others, whole = weight_refs(plan, "attend", refs[:a])
    own, send, dx, sums, w, d_mixed, d_qkv, sem_w = refs[a:]
    width = plan.width
    first = ids[0] == 0
    start_weights(plan, layer, "attend", ids, shard, others, whole, w, sem_w)
    d = d_resid[...].astype(jnp.bfloat16)
    split(first, own, send, 3 * BLOCK, d)
    wait_all(w, sem_w)
    d_mixed[...] = mm(d, w[3], 1, 1).astype(jnp.bfloat16)

    def tile(t, carry):
        at = pl.multiple_of(t * LANES, LANES)
        q = qkv[:, pl.ds(at, LANES)]
        k = qkv[:, pl.ds(width + at, LANES)]
        v = qkv[:, pl.ds(2 * width + at, LANES)]
        dm = d_mixed[:, pl.ds(at, LANES)]
        dq = dk = dv = None
        for h in range(2):
            p = probs[2 * t + h]
            dm_h = head_of(dm, h)
            dv_h = mm(p.astype(jnp.bfloat16), dm_h, 0, 0)
            dp = mm(dm_h, v, 1, 1)
            ds = p * (dp - jnp.sum(dp * p, axis=-1, keepdims=True))
            ds = ds.astype(jnp.bfloat16)
            dq_h = mm(ds, head_of(k, h), 1, 0)
            dk_h = mm(ds, head_of(q, h), 0, 0)
            dq = dq_h if dq is None else dq + dq_h
            dk = dk_h if dk is None else dk + dk_h
            dv = dv_h if dv is None else dv + dv_h
        scale = HEAD_DIM ** (-0.5)
        dq = dq * scale
        dk = dk * scale
        dq = dq * cosv[...] - swap_halves(dq) * sinv[...]
        dk = dk * cosv[...] - swap_halves(dk) * sinv[...]
        d_qkv[:, pl.ds(at, LANES)] = dq.astype(jnp.bfloat16)
        d_qkv[:, pl.ds(width + at, LANES)] = dk.astype(jnp.bfloat16)
        d_qkv[:, pl.ds(2 * width + at, LANES)] = dv.astype(jnp.bfloat16)
        return carry

    lax.fori_loop(0, width // LANES, tile, 0)
    total = None
    for j in range(3):
        part_in = d_qkv[:, j * width : (j + 1) * width]
        split(first, own, send, j * BLOCK, part_in)
        part = mm(part_in, w[j], 1, 1)
        total = part if total is None else total + part
    hat, scale = normalize(x_ref[...].astype(jnp.float32))
    sums[0:1, :] = jnp.sum(total * hat, axis=0, keepdims=True)
    sums[1:2, :] = jnp.sum(total, axis=0, keepdims=True)
    back = (d_resid[...] + norm_backward(total, hat, scale, small[0:1, :])).astype(jnp.bfloat16)
    dx[...] = back
    split(first, own, send, 4 * BLOCK, back)


def pack(plan, ids, qkv, out, up, down, keep, send):
    width, tall = plan.width, plan.tall
    first = ids[0] == 0
    at = 0
    for ref in (qkv, out, up, down):
        for b in range(PARTS if ref is down else ref.shape[2] // width):
            if ref is down:
                block = ref[0, b * tall : (b + 1) * tall, :]
            else:
                block = ref[0, :, b * width : (b + 1) * width]
            low, high = block[:, :BLOCK], block[:, BLOCK:]
            keep[at] = jnp.where(first, low, high)
            send[at] = jnp.where(first, high, low)
            at += 1


def final_layout(plan, kind, ids, low_own, low_got, high_own, high_got, *outs):
    width, tall = plan.width, plan.tall
    group = ids[1]
    first = ids[0] == 0
    tables = masks_of(plan.groups, False)
    for h, (a, b) in enumerate(((low_own, high_got), (low_got, high_own))):
        for j in range(plan.groups):
            peer = group ^ tables[h][j]
            for p in range(PARTS):
                value = jnp.where(first, a[j, p], b[j, p]).astype(jnp.float32)
                if kind == "down":
                    at = pl.multiple_of(peer * (tall * PARTS) + p * tall, 8)
                    outs[0][0, pl.ds(at, tall), h * BLOCK : (h + 1) * BLOCK] = value
                    continue
                at = pl.multiple_of(peer * tall, 8)
                out = outs[-1] if kind == "attend" and p == PARTS - 1 else outs[0]
                c = 0 if kind == "attend" and p == PARTS - 1 else p
                lanes = slice(c * width + h * BLOCK, c * width + (h + 1) * BLOCK)
                out[0, pl.ds(at, tall), lanes] = value


SHARDS = {"attend": 2, "up": 1, "down": 1}


def plan_inputs(plan, kind):
    return 2 * SHARDS[kind] + 4 if plan.direct else 1


def weight_refs(plan, kind, refs):
    if not plan.direct:
        return None, None, refs[0]
    n = SHARDS[kind]
    return (refs[:n], refs[n : 2 * n]), refs[2 * n :], None


DEPTH = 2
DEPTH_BACK = 9
EARLY = "down"
LATE = 2
GATHERS = {"upper": (1, ("down", "up", "attend")), "feed": (0, ("down", "up")), "attend": (0, ("attend",))}
SHIFT = 1
OLD = False
BESIDE = 0
ROWS_FIRST = ((1, "down"),)

VMEM = pl.BlockSpec(memory_space=pltpu.VMEM)
SMEM = pl.BlockSpec(memory_space=pltpu.SMEM)
HBM = pl.BlockSpec(memory_space=pl.ANY)


def call(body, name, args, specs, outs, out_specs, scratch, flops):
    moved = sum(x.size * x.dtype.itemsize for x in list(args) + list(outs))
    return pl.pallas_call(
        body,
        out_shape=outs,
        in_specs=specs,
        out_specs=out_specs,
        scratch_shapes=scratch,
        name=name,
        cost_estimate=pl.CostEstimate(flops=flops, transcendentals=0, bytes_accessed=moved),
        compiler_params=pltpu.CompilerParams(vmem_limit_bytes=58 << 20),
    )(*args)


def shape(dims, dtype):
    return jax.ShapeDtypeStruct(dims, dtype)


BF, F32 = jnp.bfloat16, jnp.float32


class Kernels:
    def __init__(self, plan, ids, lens, tables, heads):
        self.plan, self.ids, self.lens, self.tables, self.heads = plan, ids, lens, tables, heads
        self.part = pltpu.VMEM((PARTS, plan.width, plan.width), BF)
        self.tall = pltpu.VMEM((PARTS * plan.width, plan.width), BF)
        self.sem = pltpu.SemaphoreType.DMA(())

    def attend_forward(self, layer, x, small, weights):
        p = self.plan
        t, d = p.tok, p.width
        return call(
            functools.partial(attend_forward, p, layer),
            f"attend_forward_{layer}",
            (self.ids, self.lens, x, small, *self.tables, *weights),
            [SMEM, SMEM] + [VMEM] * 4 + [HBM] * len(weights),
            (
                shape((t, 3 * d), BF),
                shape((self.heads, t, t), F32),
                shape((t, 2 * d), BF),
                shape((t, d), F32),
            ),
            (VMEM,) * 4,
            [self.part, pltpu.VMEM((t, t), F32), self.sem],
            2 * t * d * d * 4 + 4 * self.heads * t * t * LANES,
        )

    def feed_forward(self, layer, resid, small, weights):
        p = self.plan
        t, d = p.tok, p.width
        return call(
            functools.partial(feed_forward, p, layer),
            f"feed_forward_{layer}",
            (self.ids, resid, small, *weights),
            [SMEM, VMEM, VMEM] + [HBM] * len(weights),
            (
                shape((t, (PARTS + 1) * d), BF),
                shape((t, PARTS * d), F32),
                shape((t, d), BF),
            ),
            (VMEM,) * 3,
            [self.part, self.tall, self.sem, self.sem],
            2 * t * d * d * 8,
        )

    def weight_grad(self, layer, kind, body, args, specs, flops):
        p = self.plan
        if not p.direct:
            dims = (PARTS * p.width, BLOCK) if kind == "down" else (PARTS, p.width, BLOCK)
            outs = (shape(dims, BF),)
        else:
            halved = (p.groups, p.rows // 2) if p.rows_first(layer, kind) else (p.groups // 2, p.rows)
            piece = (p.tall * PARTS, BLOCK) if kind == "down" else (PARTS, p.tall, BLOCK)
            outs = (shape((*halved, *piece), BF),) * 2
        dims = (PARTS * p.width, BLOCK) if kind == "down" else (PARTS, p.width, BLOCK)
        return pl.pallas_call(
            body,
            out_shape=outs,
            grid_spec=pltpu.PrefetchScalarGridSpec(
                num_scalar_prefetch=1,
                grid=(1,),
                in_specs=specs,
                out_specs=(HBM,) * len(outs),
                scratch_shapes=[pltpu.VMEM(dims, BF), self.sem],
            ),
            name=f"{kind}_grad_{layer}",
            cost_estimate=pl.CostEstimate(flops=flops, transcendentals=0, bytes_accessed=1 << 22),
        )(self.ids, *args)

    def down_grad(self, layer, acts, d, at):
        p = self.plan
        left = pl.BlockSpec((p.tok, PARTS * p.width), lambda i, ids: (0, 0))
        right = pl.BlockSpec(d[0].shape, lambda i, ids: (0, 0))
        flops = 4 * p.tok * p.width * PARTS * BLOCK
        return self.weight_grad(
            layer, "down", functools.partial(down_grad, p, p.rows_first(layer, "down"), at), (*acts, *d), [left] * 2 + [right] * 2, flops
        )

    def up_grad(self, layer, acts, d):
        p = self.plan
        left = pl.BlockSpec((p.tok, p.width), lambda i, ids: (0, PARTS))
        right = pl.BlockSpec(d[0].shape, lambda i, ids: (0, 0))
        flops = 4 * p.tok * p.width * PARTS * BLOCK
        return self.weight_grad(
            layer, "up", functools.partial(up_grad, p, p.rows_first(layer, "up")), (*acts, *d), [left] * 2 + [right] * 2, flops
        )

    def attend_grad(self, layer, acts, d):
        p = self.plan
        left = pl.BlockSpec(acts[0].shape, lambda i, ids: (0, 0))
        right = pl.BlockSpec(d[0].shape, lambda i, ids: (0, 0))
        flops = 4 * p.tok * p.width * PARTS * BLOCK
        return self.weight_grad(
            layer, "attend", functools.partial(attend_grad, p, p.rows_first(layer, "attend")), (*acts, *d), [left] * 2 + [right] * 2, flops
        )

    def feed_backward(self, layer, d_out, resid, slope, small, weights):
        p = self.plan
        t, d = p.tok, p.width
        return call(
            functools.partial(feed_backward, p, layer),
            f"feed_backward_{layer}",
            (self.ids, d_out, resid, slope, small, *weights),
            [SMEM] + [VMEM] * 4 + [HBM] * len(weights),
            (*(shape((t, PARTS * BLOCK), BF),) * 2, shape((t, d), F32), shape((2, d), F32)),
            (VMEM,) * 4,
            [self.part, self.tall, self.sem, self.sem],
            2 * t * d * d * 8,
        )

    def attend_backward(self, layer, x, d_resid, qkv, probs, small, weights):
        p = self.plan
        t, d = p.tok, p.width
        return call(
            functools.partial(attend_backward, p, layer),
            f"attend_backward_{layer}",
            (self.ids, x, d_resid, qkv, probs, small, *self.tables, *weights),
            [SMEM] + [VMEM] * 7 + [HBM] * len(weights),
            (*(shape((t, (PARTS + 1) * BLOCK), BF),) * 2, shape((t, d), BF), shape((2, d), F32)),
            (VMEM,) * 4,
            [self.part, pltpu.VMEM((t, d), BF), pltpu.VMEM((t, 3 * d), BF), self.sem],
            2 * t * d * d * 4 + 10 * self.heads * t * t * LANES,
        )

    def pack(self, shards):
        p = self.plan
        dims = (3 * PARTS, p.tall, BLOCK)
        specs = []
        for i, w in enumerate(shards):
            tall = p.tall * PARTS if i == len(shards) - 1 else p.tall
            specs.append(pl.BlockSpec((1, tall, w.shape[2]), lambda i, ids: (0, ids[1], 0)))
        whole = pl.BlockSpec(dims, lambda i, ids: (0, 0, 0))
        return pl.pallas_call(
            functools.partial(pack, p),
            out_shape=(shape(dims, BF),) * 2,
            grid_spec=pltpu.PrefetchScalarGridSpec(
                num_scalar_prefetch=1, grid=(1,), in_specs=specs, out_specs=(whole, whole)
            ),
            name="pack",
        )(self.ids, *shards)

    def final(self, kind, sources):
        p = self.plan
        share, d = p.width // p.rows, p.width
        dims = {"attend": ((share, 3 * d), (share, d)), "up": ((share, PARTS * d),), "down": ((share * PARTS, d),)}
        outs = tuple(shape((1, *dim), F32) for dim in dims[kind])
        specs = []
        for x, at in sources:
            specs.append(pl.BlockSpec((p.groups, PARTS, p.tall, BLOCK), lambda i, ids, at=at: (0, at, 0, 0)))
        return pl.pallas_call(
            functools.partial(final_layout, p, kind),
            out_shape=outs,
            grid_spec=pltpu.PrefetchScalarGridSpec(
                num_scalar_prefetch=1,
                grid=(1,),
                in_specs=specs,
                out_specs=tuple(pl.BlockSpec(o.shape, lambda i, ids: (0, 0, 0)) for o in outs),
            ),
            name=f"final_{kind}",
        )(self.ids, *(x for x, _ in sources))


def swap_cores(x):
    return lax.ppermute(x, "section", [(0, 1), (1, 0)])


def stage_bits(groups):
    bits = [1 << i for i in range(groups.bit_length() - 1)]
    turn = len(bits) // 2
    return bits, bits[turn:] + bits[:turn]


def swap_groups(x, groups, stage):
    pairs = []
    for core, bits in enumerate(stage_bits(groups)):
        pairs += [(core * groups + g, core * groups + (g ^ bits[stage])) for g in range(groups)]
    return lax.ppermute(x, ("section", "group"), pairs)


def along(x, distance):
    rows = lax.axis_size("dp")
    return lax.ppermute(x, "dp", [(i, (i + distance) % rows) for i in range(rows)])


def gate(x, after):
    return lax.optimization_barrier((x, *after))[0] if after else x


def swap_rows(x, bit):
    rows = lax.axis_size("dp")
    return lax.ppermute(x, "dp", [(i, i ^ bit) for i in range(rows)])


KINDS = ("attend", "up", "down")


def piece_of(plan, group, kind, shards):
    tall = plan.tall

    def cut(w, inside):
        if inside:
            w = lax.dynamic_slice_in_dim(w[0], group * (tall * PARTS), tall * PARTS, 0)
            return w.reshape(PARTS, tall, 2, BLOCK).transpose(2, 0, 1, 3)
        w = lax.dynamic_slice_in_dim(w[0], group * tall, tall, 0)
        return w.reshape(tall, -1, 2, BLOCK).transpose(2, 1, 0, 3)

    return jnp.concatenate([cut(w, kind == "down") for w in shards], axis=1)


def whole_of(plan, core, group, row, kind, shard, half_mine, half_theirs):
    groups, rows, tall = plan.groups, plan.rows, plan.tall
    tables = jnp.array(masks_of(groups, True), jnp.int32)
    first = core == 0
    halves = []
    for h in range(2):
        got = jnp.where(core == h, half_mine, half_theirs)
        got = jnp.take(got, jnp.argsort(group ^ tables[h]), axis=0)
        own = []
        for w in shard:
            if kind == "down":
                w = w[0].reshape(groups, PARTS, tall, 2, BLOCK)[:, :, :, h]
            else:
                w = w[0].reshape(groups, tall, -1, 2, BLOCK)[:, :, :, h].transpose(0, 2, 1, 3)
            own.append(w)
        own = jnp.concatenate(own, axis=1)[:, None]
        got = jnp.concatenate([got, own], axis=1)
        held = jnp.stack([row_from(plan, row, k) for k in range(rows - 1)] + [row])
        got = jnp.take(got, jnp.argsort(held), axis=1)
        if kind == "down":
            halves.append(got.transpose(1, 0, 2, 3, 4).reshape(PARTS * plan.width, BLOCK))
        else:
            halves.append(got.transpose(2, 1, 0, 3, 4).reshape(PARTS, plan.width, BLOCK))
    return jnp.stack(halves)


def ordered_grads(plan, kind, core, group, row, x):
    groups, rows, tall = plan.groups, plan.rows, plan.tall
    tables = jnp.array(masks_of(groups, False), jnp.int32)
    if kind == "down":
        x = x.reshape(rows, groups, PARTS, tall, BLOCK).transpose(1, 0, 2, 3, 4)
    else:
        x = x.reshape(PARTS, rows, groups, tall, BLOCK).transpose(2, 1, 0, 3, 4)
    x = jnp.take(x, group ^ jnp.where(core == 0, tables[0], tables[1]), axis=0)
    x = jnp.take(x, jnp.stack([row_to(plan, row, k) for k in range(rows)]), axis=1)
    return x[: groups // 2], x[groups // 2 :]


def on_device(
    tokens,
    cotangent,
    lengths,
    attend_gain,
    attend_bias,
    qkv_weight,
    out_weight,
    feed_gain,
    feed_bias,
    up_weight,
    down_weight,
):
    core = lax.axis_index("section")
    group = lax.axis_index("group")
    row = lax.axis_index("dp")
    groups = lax.axis_size("group")
    rows = lax.axis_size("dp")
    stages = groups.bit_length() - 1
    tok, width = tokens.shape[1:]
    plan = Plan(groups, rows, tok, width)
    few = plan.few
    first = core == 0
    share = width // rows
    ids = jnp.stack([core, group, row]).astype(jnp.int32)
    lens = lax.dynamic_index_in_dim(lengths, core, 0, False)[0]

    shards = {"attend": (qkv_weight, out_weight), "up": (up_weight,), "down": (down_weight,)}
    chunks = [(layer, kind) for layer in range(2) for kind in KINDS]
    n_chunks = len(chunks)
    x0 = lax.dynamic_index_in_dim(tokens, core, 0, False)
    cot = lax.dynamic_index_in_dim(cotangent, core, 0, False)
    cosine, sine, _ = rope_tables(lens, tok)
    kernels = Kernels(plan, ids, lens, (cosine, sine), width // HEAD_DIM)
    history = {}
    pieces, bufs, gots, theirs, saved = {}, {}, {}, {}, {}
    xs = {0: x0}
    small = jnp.stack([attend_gain[0], attend_bias[0], feed_gain[0], feed_bias[0]])[None]

    if plan.direct:
        keep, send = kernels.pack([w for kind in KINDS for w in shards[kind]])
    else:
        both = jnp.concatenate([piece_of(plan, group, kind, shards[kind]) for kind in KINDS], axis=1)
        keep = lax.dynamic_index_in_dim(both, core, 0, False)
        send = lax.dynamic_index_in_dim(both, 1 - core, 0, False)
    got = swap_cores(send)
    for layer in range(2):
        part = jnp.where(core == layer, keep, got)
        for i, kind in enumerate(KINDS):
            pieces[layer, kind] = part[i * PARTS : (i + 1) * PARTS][None, None]

    def weights_of(layer, kind):
        parts = [*bufs[layer, kind], *gots[layer, kind]]
        if plan.direct:
            if kind == "down":
                parts = [p.reshape(*p.shape[:2], PARTS * plan.tall, BLOCK) for p in parts]
            return (*shards[kind], *theirs[kind], *parts)
        mine, other = (jnp.concatenate(p, axis=0) for p in (parts[:2], parts[2:]))
        shard = [jnp.where(core == layer, a, b) for a, b in zip(shards[kind], theirs[kind])]
        return (whole_of(plan, core, group, row, kind, shard, mine, other),)

    def run_attend(layer, after):
        x = gate(xs[layer], after)
        out = kernels.attend_forward(layer, x, smalls[layer], weights_of(layer, "attend"))
        saved[layer, "attend"] = out
        return out[3]

    def run_feed(layer, after):
        resid = gate(saved[layer, "attend"][3], after)
        weights = weights_of(layer, "up") + weights_of(layer, "down")
        *out, y = kernels.feed_forward(layer, resid, smalls[layer], weights)
        saved[layer, "feed"] = out
        xs[layer + 1] = y
        return y

    row_bits = [1 << i for i in range(rows.bit_length() - 1)]
    hops = len(row_bits) if few else 1
    depth = hops + stages
    kernel_at = {depth + SHIFT: (run_attend, 0), depth + 2 + SHIFT: (run_feed, 0), depth + 3 + SHIFT: (run_attend, 1)}
    small_steps = row_bits + [0]
    gotten, to_swap, acts_too = {}, {}, {}
    for slot in range(n_chunks + depth + 1):
        after = history.get(slot - DEPTH, [])
        done = []
        for stage in range(depth, -1, -1):
            c = slot - stage
            if not 0 <= c < n_chunks:
                continue
            chunk = chunks[c]
            if stage == depth:
                gots[chunk].append(swap_cores(gate(bufs[chunk][1], after)))
                done.append(gots[chunk][-1])
                continue
            if stage < hops:
                piece = pieces[chunk]
                if few:
                    got = swap_rows(gate(piece, after), row_bits[hops - 1 - stage])
                    pieces[chunk] = jnp.concatenate([piece, got], axis=1)
                    gotten.setdefault(chunk, []).append(got)
                else:
                    got = lax.all_gather(gate(piece[0, 0], after), "dp")
                    back = (row - 1 - jnp.arange(rows - 1)) % rows
                    gotten[chunk] = [jnp.take(got, back, axis=0)[None]]
                done.append(got)
                continue
            if stage == hops:
                bufs[chunk] = jnp.concatenate(gotten[chunk], axis=1)
            buf = bufs[chunk]
            got = swap_groups(gate(buf, after), groups, stage - hops)
            done.append(got)
            if stage + 1 < depth:
                bufs[chunk] = jnp.concatenate([buf, got], axis=0)
            else:
                bufs[chunk] = [buf, got]
                gots[chunk] = [swap_cores(gate(buf, after))]
                done.append(gots[chunk][0])
        if few and slot < len(small_steps):
            bit = small_steps[slot]
            held = gate(small, history.get(slot - 1, []))
            got = swap_rows(held, bit) if bit else swap_cores(held)
            done.append(got)
            small = jnp.concatenate([small, got])
        elif slot == 0:
            small = lax.all_gather(small, ("section", "dp"))
        if slot == (len(small_steps) if few else 1):
            got = small.reshape(2, rows, PARTS, share)
            if few:
                got = jnp.take(got, row ^ jnp.arange(rows), axis=1)
                got = jnp.take(got, core ^ jnp.arange(2), axis=0)
            smalls = got.transpose(0, 2, 1, 3).reshape(2, PARTS, width).astype(F32)
        if 1 <= slot <= len(KINDS):
            kind = KINDS[slot - 1]
            theirs[kind] = tuple(swap_cores(gate(w, history[slot - 1])) for w in shards[kind])
            done += theirs[kind]
        for (layer, kind), acts in list(to_swap.items()):
            acts_too[layer, kind] = swap_cores(gate(acts, after))
            done.append(acts_too[layer, kind])
            del to_swap[layer, kind]
        if slot in kernel_at:
            run, layer = kernel_at[slot]
            done.append(run(layer, history[slot - 1]))
            if run is run_attend:
                to_swap[layer, "attend"] = saved[layer, "attend"][2]
            else:
                to_swap[layer, "feed"] = saved[layer, "feed"][0]
        history[slot] = done
    run_feed(1, [])
    to_swap[1, "feed"] = saved[1, "feed"][0]
    for (layer, kind), acts in to_swap.items():
        acts_too[layer, kind] = swap_cores(acts)

    backs, sums, d_cols = [None, None], {}, {}
    order = [(layer, kind) for layer in (1, 0) for kind in ("down", "up", "attend")]
    halves = lax.dynamic_slice_in_dim(cotangent, core * BLOCK, BLOCK, 2)
    d_cols[2, "attend"] = (
        lax.dynamic_index_in_dim(halves, core, 0, False),
        lax.dynamic_index_in_dim(halves, 1 - core, 0, False),
    )
    d_outs = {1: cot}
    d_resids = {}

    def chain_feed(layer, after):
        weights = weights_of(layer, "up") + weights_of(layer, "down")
        resid, slope = saved[layer, "attend"][3], saved[layer, "feed"][1]
        own, send, d_resids[layer], sums[layer, "up"] = kernels.feed_backward(
            layer, gate(d_outs[layer], after), resid, slope, smalls[layer], weights
        )
        d_cols[layer, "up"] = (own, swap_cores(send))
        return send

    def chain_attend(layer, after):
        qkv, probs = saved[layer, "attend"][:2]
        own, send, dx, sums[layer, "attend"] = kernels.attend_backward(
            layer,
            xs[layer],
            gate(d_resids[layer], after),
            qkv,
            probs,
            smalls[layer],
            weights_of(layer, "attend"),
        )
        d_cols[layer, "attend"] = (own, swap_cores(send))
        backs[layer] = d_outs[layer - 1] = dx
        return send

    def weight_grad(layer, kind, after):
        if kind == "attend":
            acts = (saved[layer, "attend"][2], acts_too[layer, "attend"])
            own, other = d_cols[layer, "attend"]
            outs = kernels.attend_grad(layer, acts, (gate(own, after), other))
        else:
            acts = (saved[layer, "feed"][0], acts_too[layer, "feed"])
            own, other = d_cols[layer, "up"] if kind == "up" else d_cols[layer + 1, "attend"]
            d = (gate(own, after), other)
            if kind == "up":
                outs = kernels.up_grad(layer, acts, d)
            else:
                outs = kernels.down_grad(layer, acts, d, 0 if layer == 1 else PARTS * BLOCK)
        if not plan.direct:
            return ordered_grads(plan, kind, core, group, row, outs[0])
        return [x.reshape(*x.shape[:2], PARTS, plan.tall, BLOCK) for x in outs]

    def total_of(parts):
        total = parts[0].astype(F32)
        for part in parts[1:]:
            total = total + part.astype(F32)
        return total.astype(BF)

    def way_of(layer, kind):
        over_groups = [(0, i) for i in range(stages)]
        over_rows = [(1, bit) for bit in row_bits] if few else [(1, 0)]
        return over_rows + over_groups if plan.rows_first(layer, kind) else over_groups + over_rows

    last = stages + hops

    def step(layer, kind, parts, stage, after):
        if stage == 0:
            send = gate(parts["send"], after)
            axis, bit = way_of(layer, kind)[0]
            got = swap_rows(send, bit) if axis else swap_groups(send, groups, bit)
            parts["sum"] = [parts["keep"], got]
            parts["left"] = list(parts["keep"].shape[:2])
            return got
        axis, bit = way_of(layer, kind)[stage]
        if axis == 1 and not few:
            send = total_of([p[0] for p in parts["sum"]])
            held = jnp.argsort(jnp.stack([row_to(plan, row, k) for k in range(rows)]))
            send = gate(jnp.take(send, held, axis=0), after)
            got = lax.psum_scatter(send, "dp", scatter_dimension=0, tiled=True)
            parts["sum"] = [got[None]]
            parts["left"] = [1, 1]
            return got
        low, high = [0, 0], list(parts["left"])
        low[axis] = high[axis] // 2
        send = total_of([p[low[0] : high[0], low[1] : high[1]] for p in parts["sum"]])
        parts["left"][axis] //= 2
        send = gate(send, after)
        sends.append(send)
        got = swap_groups(send, groups, bit) if axis == 0 else swap_rows(send, bit)
        parts["sum"] = parts["sum"] + [got]
        return got

    def result_of(parts):
        return total_of([p[:1, 0] for p in parts["sum"]])

    def home(low, high):
        got = swap_cores(jnp.where(first, high, low))
        keep = jnp.where(first, low, high)
        return jnp.where(first, jnp.stack([keep, got]), jnp.stack([got, keep]))

    layer_out = home(xs[1], xs[2])
    history, sends = {}, []
    chain_feed(1, [])
    keep, send = weight_grad(*order[0], [])
    live = {0: {"keep": keep, "send": send}}
    def outside(x):
        return x.transpose(0, 3, 2, 1, 4).reshape(1, share, -1).astype(F32)

    def result_for(kind):
        sources = []
        for source_layer in range(2):
            for name, (layer, kinds) in gathers.items():
                if layer == source_layer and kind in kinds:
                    sources += [(x, kinds.index(kind)) for x in final[name]]
        if plan.direct:
            return kernels.final(kind, sources)
        parts = [x[:, i * PARTS : (i + 1) * PARTS] for x, i in sources]
        tables = jnp.array(masks_of(groups, False), jnp.int32)
        low = jnp.take(jnp.where(first, parts[0], parts[3]), jnp.argsort(group ^ tables[0]), axis=0)
        high = jnp.take(jnp.where(first, parts[1], parts[2]), jnp.argsort(group ^ tables[1]), axis=0)
        x = jnp.stack([low, high], axis=1)
        if kind == "attend":
            return (outside(x[:, :, 0:3]), outside(x[:, :, 3:4]))
        if kind == "up":
            return (outside(x),)
        return (x.transpose(0, 2, 3, 1, 4).reshape(1, -1, width).astype(F32),)

    final, results = {}, {}
    gathers = GATHERS
    small_sum, small_stage, smalls_seen = None, 0, []
    beside = [[(chain_attend, 1)], [(chain_feed, 0)], [(chain_attend, 0)], [], []]
    for slot in range(n_chunks + last + stages + 1):
        after = history.get(slot - DEPTH_BACK, [])
        done = []
        sends.clear()
        for c in range(n_chunks):
            if 0 <= slot - c < last:
                held = smalls_seen[-LATE : len(smalls_seen) - LATE + 1] if LATE and c == n_chunks - 1 else []
                done.append(step(*order[c], live[c], slot - c, after + held))
        for name, (layer, kinds) in gathers.items():
            stage = slot - last - max(order.index((layer, kind)) for kind in kinds)
            if stage == 0:
                final[name] = jnp.concatenate([result_of(live[order.index((layer, k))]) for k in kinds], axis=1)
            if 0 <= stage < stages:
                got = swap_groups(final[name], groups, stages - 1 - stage)
                final[name] = jnp.concatenate([final[name], got], axis=0)
            elif stage == stages:
                held = final[name]
                if name == "attend":
                    held = gate(held, [layer_out, input_grad, *results[EARLY]] if EARLY else [layer_out, input_grad])
                got = lax.ppermute(held, "section", [(1 - layer, layer)])
                final[name] = (final[name], got)
                if name == "feed":
                    for kind in ("down", "up"):
                        results[kind] = result_for(kind)
        if slot + 1 < n_chunks:
            before = history.get(slot - 1, []) if OLD else list(sends)
            now = done[-BESIDE:] if BESIDE else []
            extra = []
            for run, layer in beside[slot]:
                if order[slot + 1][1] == "down":
                    continue
                extra.append(run(layer, before))
            keep, send = weight_grad(*order[slot + 1], extra or before)
            live[slot + 1] = {"keep": keep, "send": gate(send, now)}
            if order[slot + 1][1] == "down":
                for run, layer in beside[slot]:
                    extra.append(run(layer, [send]))
            if OLD:
                done.append(send)
        if slot + 1 == n_chunks:
            input_grad = home(*backs)
            small_sum = jnp.stack([jnp.concatenate([sums[i, "attend"], sums[i, "up"]]) for i in range(2)])
        if small_sum is not None and small_stage <= stages + len(row_bits):
            held = gate(small_sum, history.get(slot - 1, []))
            if small_stage == 0:
                got = swap_cores(held)
            elif small_stage <= stages:
                got = swap_groups(held, groups, small_stage - 1)
            else:
                got = swap_rows(held, row_bits[small_stage - stages - 1])
            small_stage += 1
            small_sum = small_sum + got
            smalls_seen.append(small_sum)
        history[slot] = done

    qkv_grad, out_grad = result_for("attend")
    (up_grad,) = results["up"]
    (down_grads,) = results["down"]

    small_grads = small_sum
    own = lax.dynamic_index_in_dim(small_grads, core, 0, False)
    own = lax.dynamic_slice_in_dim(own, row * share, share, 1)
    return (
        layer_out[None],
        input_grad[None],
        own[0][None],
        own[1][None],
        qkv_grad,
        out_grad,
        own[2][None],
        own[3][None],
        up_grad,
        down_grads,
    )


def solution(mesh):
    placed = (
        P(None, ("group", "dp"), None),
        P(None, ("group", "dp"), None),
        P(None, ("group", "dp"), None),
        P("section", "dp"),
        P("section", "dp"),
        P("section", "dp", None),
        P("section", "dp", None),
        P("section", "dp"),
        P("section", "dp"),
        P("section", "dp", None),
        P("section", "dp", None),
    )
    return jax.shard_map(
        on_device,
        mesh=mesh,
        in_specs=placed,
        out_specs=(
            P("section", None, ("group", "dp"), None),
            P("section", None, ("group", "dp"), None),
            P("section", "dp"),
            P("section", "dp"),
            P("section", "dp", None),
            P("section", "dp", None),
            P("section", "dp"),
            P("section", "dp"),
            P("section", "dp", None),
            P("section", "dp", None),
        ),
        check_vma=False,
    )
```

```python
import functools

import jax
import jax.numpy as jnp
from jax import lax
from jax.experimental import pallas as pl
from jax.experimental.pallas import tpu as pltpu
from jax.sharding import PartitionSpec as P

HEAD_DIM = 64
LANES = 128
BLOCK = 384
PARTS = 4


masked_score = -1000000000.0


def rope_tables(lengths_row, tok):
    bounds = jnp.cumsum(lengths_row, dtype=jnp.int32)
    places = jnp.arange(tok, dtype=jnp.int32)
    segment = jnp.sum((places[:, None] >= bounds[None, :-1]).astype(jnp.int32), axis=1)
    starts = bounds - lengths_row
    picks = jnp.arange(lengths_row.shape[0], dtype=jnp.int32)
    begin = jnp.sum(jnp.where(segment[:, None] == picks[None, :], starts[None, :], 0), axis=1)
    offset = (places - begin).astype(jnp.float32)
    half = HEAD_DIM // 2
    freqs = 10000.0 ** (-jnp.arange(half, dtype=jnp.float32) / half)
    angles = offset[:, None] * freqs[None, :]
    cosine, sine = jnp.cos(angles), jnp.sin(angles)
    heads = LANES // HEAD_DIM
    cosine = jnp.concatenate([cosine, cosine] * heads, axis=1)
    sine = jnp.concatenate([-sine, sine] * heads, axis=1)
    return cosine, sine, segment


def mm(left, right, left_dim, right_dim):
    return lax.dot_general(
        left, right, (((left_dim,), (right_dim,)), ((), ())), preferred_element_type=jnp.float32
    )


def normalize(x):
    center = x - jnp.mean(x, axis=-1, keepdims=True)
    spread = jnp.mean(center * center, axis=-1, keepdims=True)
    scale = lax.rsqrt(spread + 1e-05)
    return center * scale, scale


def norm_backward(d_out, hat, scale, gain):
    d_hat = d_out * gain
    part = d_hat - jnp.mean(d_hat, axis=-1, keepdims=True)
    part = part - hat * jnp.mean(d_hat * hat, axis=-1, keepdims=True)
    return part * scale


def swap_halves(x):
    half = HEAD_DIM // 2
    lane = lax.broadcasted_iota(jnp.int32, x.shape, 1)
    low = lane % HEAD_DIM < half
    return jnp.where(low, pltpu.roll(x, LANES - half, 1), pltpu.roll(x, half, 1))


def head_of(x, which):
    lane = lax.broadcasted_iota(jnp.int32, x.shape, 1)
    inside = lane < HEAD_DIM if which == 0 else lane >= HEAD_DIM
    return jnp.where(inside, x, jnp.zeros_like(x))


def masks_of(groups, low_first):
    bits = [1 << i for i in range(groups.bit_length() - 1)]
    turn = len(bits) // 2
    tables = []
    for order in (bits, bits[turn:] + bits[:turn]):
        if not low_first:
            order = order[::-1]
        tables.append([sum(b for t, b in enumerate(order) if (j >> t) & 1) for j in range(groups)])
    return tables


def row_masks(rows):
    bits = [1 << i for i in reversed(range(rows.bit_length() - 1))]
    return [sum(b for t, b in enumerate(bits) if (k >> t) & 1) for k in range(rows)]


def row_to(plan, row, k):
    return row ^ row_masks(plan.rows)[k] if plan.few else (row + k) % plan.rows


def row_from(plan, row, k):
    if plan.few:
        return row ^ row_masks(plan.rows)[k + 1]
    return (row + (plan.rows - 1 - k)) % plan.rows


def pick(flag, a, b):
    return a if a == b else jnp.where(flag, a, b)


class Plan:
    def __init__(self, groups, rows, tok, width):
        self.groups = groups
        self.rows = rows
        self.tok = tok
        self.width = width
        self.pieces = groups * rows
        self.tall = width // self.pieces
        self.direct = self.tall % 16 == 0
        self.few = rows <= 4 and rows & (rows - 1) == 0

    def rows_first(self, layer, kind):
        return self.few and self.direct and (layer, kind) in ROWS_FIRST


def start_weights(plan, layer, kind, ids, own, others, whole, dst, sem):
    width, tall = plan.width, plan.tall
    if not plan.direct:
        for h in range(2):
            lanes = pl.ds(h * BLOCK, BLOCK)
            if kind == "down":
                pltpu.make_async_copy(whole.at[h], dst.at[:, lanes], sem).start()
            else:
                pltpu.make_async_copy(whole.at[h], dst.at[:, :, lanes], sem).start()
        return
    core, group, row = ids[0], ids[1], ids[2]
    share = width // plan.rows
    mine, theirs = own

    def from_shard(refs):
        if kind == "down":
            at = pl.multiple_of(row * (share * PARTS), 16)
            pltpu.make_async_copy(refs[0].at[0], dst.at[pl.ds(at, share * PARTS)], sem).start()
            return
        at = pl.multiple_of(row * share, 16)
        j = 0
        for ref in refs:
            for b in range(ref.shape[2] // width):
                pltpu.make_async_copy(
                    ref.at[0, :, pl.ds(b * width, width)], dst.at[j, pl.ds(at, share)], sem
                ).start()
                j += 1

    @pl.when(core == layer)
    def _():
        from_shard(mine)

    @pl.when(core != layer)
    def _():
        from_shard(theirs)

    tables = masks_of(plan.groups, True)
    for half, flag, sources in ((core, core == 0, others[:2]), (1 - core, core != 0, others[2:])):
        lanes = pl.ds(pl.multiple_of(half * BLOCK, LANES), BLOCK)
        for j in range(plan.groups):
            peer = group ^ pick(flag, tables[0][j], tables[1][j])
            source = sources[j // (plan.groups // 2)]
            for k in range(plan.rows - 1):
                at = row_from(plan, row, k) * plan.groups + peer
                if kind == "down":
                    at = pl.multiple_of(at * (tall * PARTS), 16)
                    to = dst.at[pl.ds(at, tall * PARTS), lanes]
                else:
                    to = dst.at[:, pl.ds(pl.multiple_of(at * tall, 16), tall), lanes]
                pltpu.make_async_copy(source.at[j % (plan.groups // 2), k], to, sem).start()


def wait_all(ref, sem):
    pltpu.make_async_copy(ref, ref, sem).wait()


def start_grads(plan, kind, ids, src, outs, sem, rows_first):
    tall = plan.tall
    core, group, row = ids[0], ids[1], ids[2]
    if not plan.direct:
        pltpu.make_async_copy(src, outs[0], sem).start()
        return
    tables = masks_of(plan.groups, False)
    half = plan.groups // 2
    for j in range(plan.groups):
        peer = group ^ pick(core == 0, tables[0][j], tables[1][j])
        for k in range(plan.rows):
            at = row_to(plan, row, k) * plan.groups + peer
            if kind == "down":
                part = src.at[pl.ds(pl.multiple_of(at * (tall * PARTS), 16), tall * PARTS)]
            else:
                part = src.at[:, pl.ds(pl.multiple_of(at * tall, 16), tall)]
            if rows_first:
                out = outs[k // (plan.rows // 2)].at[j, k % (plan.rows // 2)]
            else:
                out = outs[j // half].at[j % half, k]
            pltpu.make_async_copy(part, out, sem).start()


def attend_forward(plan, layer, ids, lens, x_ref, small, cosv, sinv, *refs):
    n = 7
    own, others, whole = weight_refs(plan, "attend", refs[: plan_inputs(plan, "attend")])
    refs = refs[plan_inputs(plan, "attend") :]
    qkv, probs, acts, resid, w, same, sem = refs
    width, tok = plan.width, plan.tok
    start_weights(plan, layer, "attend", ids, own, others, whole, w, sem)
    x = x_ref[...].astype(jnp.float32)
    hat, _ = normalize(x)
    low = (hat * small[0:1, :] + small[1:2, :]).astype(jnp.bfloat16)
    acts[:, :width] = low
    first_end = lens[0]
    second_end = lens[0] + lens[1]

    def seg(axis):
        at = lax.broadcasted_iota(jnp.int32, (tok, tok), axis)
        return (at >= first_end).astype(jnp.int32) + (at >= second_end).astype(jnp.int32)

    same[...] = (seg(0) == seg(1)).astype(jnp.float32)
    wait_all(w, sem)
    for j in range(3):
        full = mm(low, w[j], 1, 0)
        if j == 2:
            qkv[:, j * width : (j + 1) * width] = full.astype(jnp.bfloat16)
            continue
        for t in range(width // LANES):
            part = full[:, t * LANES : (t + 1) * LANES]
            part = part * cosv[...] + swap_halves(part) * sinv[...]
            qkv[:, j * width + t * LANES : j * width + (t + 1) * LANES] = part.astype(jnp.bfloat16)

    def tile(t, carry):
        at = pl.multiple_of(t * LANES, LANES)
        q = qkv[:, pl.ds(at, LANES)]
        k = qkv[:, pl.ds(width + at, LANES)]
        v = qkv[:, pl.ds(2 * width + at, LANES)]
        total = None
        for h in range(2):
            scores = mm(head_of(q, h), k, 1, 1) * HEAD_DIM ** (-0.5)
            scores = jnp.where(same[...] > 0.5, scores, masked_score)
            peak = jnp.max(scores, axis=-1, keepdims=True)
            expd = jnp.exp(scores - peak)
            p = expd * (1.0 / jnp.sum(expd, axis=-1, keepdims=True))
            probs[2 * t + h] = p
            part = mm(p.astype(jnp.bfloat16), head_of(v, h), 1, 0)
            total = part if total is None else total + part
        acts[:, pl.ds(width + at, LANES)] = total.astype(jnp.bfloat16)
        return carry

    lax.fori_loop(0, width // LANES, tile, 0)
    resid[...] = x + mm(acts[:, width:], w[3], 1, 0)


def feed_forward(plan, layer, ids, resid, small, *refs):
    a = plan_inputs(plan, "up")
    b = plan_inputs(plan, "down")
    up_refs = weight_refs(plan, "up", refs[:a])
    down_refs = weight_refs(plan, "down", refs[a : a + b])
    acts, slope, y, wu, wd, sem_u, sem_d = refs[a + b :]
    width = plan.width
    start_weights(plan, layer, "up", ids, *up_refs, wu, sem_u)
    start_weights(plan, layer, "down", ids, *down_refs, wd, sem_d)
    hat, _ = normalize(resid[...])
    low = (hat * small[2:3, :] + small[3:4, :]).astype(jnp.bfloat16)
    acts[:, PARTS * width :] = low
    wait_all(wu, sem_u)
    total = resid[...]
    for j in range(PARTS):
        v = mm(low, wu[j], 1, 0)
        cdf = 0.5 * (1.0 + lax.erf(v * (2.0**-0.5)))
        act = (v * cdf).astype(jnp.bfloat16)
        lanes = slice(j * width, (j + 1) * width)
        acts[:, lanes] = act
        slope[:, lanes] = cdf + v * (jnp.exp(v * v * -0.5) * 0.3989422804014327)
        if j == 0:
            wait_all(wd, sem_d)
        total = total + mm(act, wd[lanes, :], 1, 0)
    y[...] = total.astype(jnp.bfloat16)


def split(first, own, send, at, x):
    low, high = x[:, :BLOCK], x[:, BLOCK:]
    own[:, at : at + BLOCK] = jnp.where(first, low, high)
    send[:, at : at + BLOCK] = jnp.where(first, high, low)


def both(own, other, lanes):
    return jnp.concatenate([own[:, lanes], other[:, lanes]], axis=0)


def down_grad(plan, rows_first, at, ids, active, active_too, d, d_too, *refs):
    *outs, g, sem = refs
    width = plan.width
    right = both(d, d_too, slice(at, at + BLOCK))
    for j in range(PARTS):
        lanes = slice(j * width, (j + 1) * width)
        g[lanes, :] = mm(both(active, active_too, lanes), right, 0, 0).astype(jnp.bfloat16)
    start_grads(plan, "down", ids, g, outs, sem, rows_first)
    wait_all(g, sem)


def up_grad(plan, rows_first, ids, normed, normed_too, d, d_too, *refs):
    *outs, g, sem = refs
    left = both(normed, normed_too, slice(0, plan.width))
    for j in range(0, PARTS, 2):
        two = mm(left, both(d, d_too, slice(j * BLOCK, (j + 2) * BLOCK)), 0, 0).astype(jnp.bfloat16)
        g[j] = two[:, :BLOCK]
        g[j + 1] = two[:, BLOCK:]
    start_grads(plan, "up", ids, g, outs, sem, rows_first)
    wait_all(g, sem)


def attend_grad(plan, rows_first, ids, acts, acts_too, d, d_too, *refs):
    *outs, g, sem = refs
    width = plan.width
    left = both(acts, acts_too, slice(0, width))
    two = mm(left, both(d, d_too, slice(0, 2 * BLOCK)), 0, 0).astype(jnp.bfloat16)
    g[0] = two[:, :BLOCK]
    g[1] = two[:, BLOCK:]
    g[2] = mm(left, both(d, d_too, slice(2 * BLOCK, 3 * BLOCK)), 0, 0).astype(jnp.bfloat16)
    left = both(acts, acts_too, slice(width, 2 * width))
    g[3] = mm(left, both(d, d_too, slice(3 * BLOCK, 4 * BLOCK)), 0, 0).astype(jnp.bfloat16)
    start_grads(plan, "attend", ids, g, outs, sem, rows_first)
    wait_all(g, sem)


def feed_backward(plan, layer, ids, d_out, resid, slope, small, *refs):
    a = plan_inputs(plan, "up")
    b = plan_inputs(plan, "down")
    up_refs = weight_refs(plan, "up", refs[:a])
    down_refs = weight_refs(plan, "down", refs[a : a + b])
    own, send, d_resid, sums, wu, wd, sem_u, sem_d = refs[a + b :]
    width = plan.width
    start_weights(plan, layer, "down", ids, *down_refs, wd, sem_d)
    start_weights(plan, layer, "up", ids, *up_refs, wu, sem_u)
    d = d_out[...]
    wait_all(wd, sem_d)
    total = None
    for j in range(PARTS):
        lanes = slice(j * width, (j + 1) * width)
        d_up = (mm(d, wd[lanes, :], 1, 1) * slope[:, lanes]).astype(jnp.bfloat16)
        split(ids[0] == 0, own, send, j * BLOCK, d_up)
        if j == 0:
            wait_all(wu, sem_u)
        part = mm(d_up, wu[j], 1, 1)
        total = part if total is None else total + part
    hat, scale = normalize(resid[...])
    sums[0:1, :] = jnp.sum(total * hat, axis=0, keepdims=True)
    sums[1:2, :] = jnp.sum(total, axis=0, keepdims=True)
    d_resid[...] = d.astype(jnp.float32) + norm_backward(total, hat, scale, small[2:3, :])


def attend_backward(plan, layer, ids, x_ref, d_resid, qkv, probs, small, cosv, sinv, *refs):
    a = plan_inputs(plan, "attend")
    shard, others, whole = weight_refs(plan, "attend", refs[:a])
    own, send, dx, sums, w, d_mixed, d_qkv, sem_w = refs[a:]
    width = plan.width
    first = ids[0] == 0
    start_weights(plan, layer, "attend", ids, shard, others, whole, w, sem_w)
    d = d_resid[...].astype(jnp.bfloat16)
    split(first, own, send, 3 * BLOCK, d)
    wait_all(w, sem_w)
    d_mixed[...] = mm(d, w[3], 1, 1).astype(jnp.bfloat16)

    def tile(t, carry):
        at = pl.multiple_of(t * LANES, LANES)
        q = qkv[:, pl.ds(at, LANES)]
        k = qkv[:, pl.ds(width + at, LANES)]
        v = qkv[:, pl.ds(2 * width + at, LANES)]
        dm = d_mixed[:, pl.ds(at, LANES)]
        dq = dk = dv = None
        for h in range(2):
            p = probs[2 * t + h]
            dm_h = head_of(dm, h)
            dv_h = mm(p.astype(jnp.bfloat16), dm_h, 0, 0)
            dp = mm(dm_h, v, 1, 1)
            ds = p * (dp - jnp.sum(dp * p, axis=-1, keepdims=True))
            ds = ds.astype(jnp.bfloat16)
            dq_h = mm(ds, head_of(k, h), 1, 0)
            dk_h = mm(ds, head_of(q, h), 0, 0)
            dq = dq_h if dq is None else dq + dq_h
            dk = dk_h if dk is None else dk + dk_h
            dv = dv_h if dv is None else dv + dv_h
        scale = HEAD_DIM ** (-0.5)
        dq = dq * scale
        dk = dk * scale
        dq = dq * cosv[...] - swap_halves(dq) * sinv[...]
        dk = dk * cosv[...] - swap_halves(dk) * sinv[...]
        d_qkv[:, pl.ds(at, LANES)] = dq.astype(jnp.bfloat16)
        d_qkv[:, pl.ds(width + at, LANES)] = dk.astype(jnp.bfloat16)
        d_qkv[:, pl.ds(2 * width + at, LANES)] = dv.astype(jnp.bfloat16)
        return carry

    lax.fori_loop(0, width // LANES, tile, 0)
    total = None
    for j in range(3):
        part_in = d_qkv[:, j * width : (j + 1) * width]
        split(first, own, send, j * BLOCK, part_in)
        part = mm(part_in, w[j], 1, 1)
        total = part if total is None else total + part
    hat, scale = normalize(x_ref[...].astype(jnp.float32))
    sums[0:1, :] = jnp.sum(total * hat, axis=0, keepdims=True)
    sums[1:2, :] = jnp.sum(total, axis=0, keepdims=True)
    back = (d_resid[...] + norm_backward(total, hat, scale, small[0:1, :])).astype(jnp.bfloat16)
    dx[...] = back
    split(first, own, send, 4 * BLOCK, back)


def pack(plan, ids, qkv, out, up, down, keep, send):
    width, tall = plan.width, plan.tall
    first = ids[0] == 0
    at = 0
    for ref in (qkv, out, up, down):
        for b in range(PARTS if ref is down else ref.shape[2] // width):
            if ref is down:
                block = ref[0, b * tall : (b + 1) * tall, :]
            else:
                block = ref[0, :, b * width : (b + 1) * width]
            low, high = block[:, :BLOCK], block[:, BLOCK:]
            keep[at] = jnp.where(first, low, high)
            send[at] = jnp.where(first, high, low)
            at += 1


def final_layout(plan, kind, ids, low_own, low_got, high_own, high_got, *outs):
    width, tall = plan.width, plan.tall
    group = ids[1]
    first = ids[0] == 0
    orders = masks_of(plan.groups, False)

    def place(j, carry):
        for h, (a, b) in enumerate(((low_own, high_got), (low_got, high_own))):
            peer = group
            for t in range(plan.groups.bit_length() - 1):
                peer = peer ^ (((j >> t) & 1) * orders[h][1 << t])
            for p in range(PARTS):
                value = jnp.where(first, a[j, p], b[j, p]).astype(jnp.float32)
                if kind == "down":
                    at = pl.multiple_of(peer * (tall * PARTS) + p * tall, 8)
                    outs[0][0, pl.ds(at, tall), h * BLOCK : (h + 1) * BLOCK] = value
                    continue
                at = pl.multiple_of(peer * tall, 8)
                out = outs[-1] if kind == "attend" and p == PARTS - 1 else outs[0]
                c = 0 if kind == "attend" and p == PARTS - 1 else p
                lanes = slice(c * width + h * BLOCK, c * width + (h + 1) * BLOCK)
                out[0, pl.ds(at, tall), lanes] = value
        return carry

    lax.fori_loop(0, plan.groups, place, 0)


SHARDS = {"attend": 2, "up": 1, "down": 1}


def plan_inputs(plan, kind):
    return 2 * SHARDS[kind] + 4 if plan.direct else 1


def weight_refs(plan, kind, refs):
    if not plan.direct:
        return None, None, refs[0]
    n = SHARDS[kind]
    return (refs[:n], refs[n : 2 * n]), refs[2 * n :], None


DEPTH = 2
DEPTH_BACK = 3
EARLY = "down"
LATE = 2
GATHERS = {"upper": (1, ("down", "up", "attend")), "feed": (0, ("down", "up")), "attend": (0, ("attend",))}
SHIFT = 1
OLD = False
BESIDE = 0
ROWS_FIRST = ((1, "down"),)

VMEM = pl.BlockSpec(memory_space=pltpu.VMEM)
SMEM = pl.BlockSpec(memory_space=pltpu.SMEM)
HBM = pl.BlockSpec(memory_space=pl.ANY)


def call(body, name, args, specs, outs, out_specs, scratch, flops):
    moved = sum(x.size * x.dtype.itemsize for x in list(args) + list(outs))
    return pl.pallas_call(
        body,
        out_shape=outs,
        in_specs=specs,
        out_specs=out_specs,
        scratch_shapes=scratch,
        name=name,
        cost_estimate=pl.CostEstimate(flops=flops, transcendentals=0, bytes_accessed=moved),
        compiler_params=pltpu.CompilerParams(vmem_limit_bytes=58 << 20),
    )(*args)


def shape(dims, dtype):
    return jax.ShapeDtypeStruct(dims, dtype)


BF, F32 = jnp.bfloat16, jnp.float32


class Kernels:
    def __init__(self, plan, ids, lens, tables, heads):
        self.plan, self.ids, self.lens, self.tables, self.heads = plan, ids, lens, tables, heads
        self.part = pltpu.VMEM((PARTS, plan.width, plan.width), BF)
        self.tall = pltpu.VMEM((PARTS * plan.width, plan.width), BF)
        self.sem = pltpu.SemaphoreType.DMA(())

    def attend_forward(self, layer, x, small, weights):
        p = self.plan
        t, d = p.tok, p.width
        return call(
            functools.partial(attend_forward, p, layer),
            f"attend_forward_{layer}",
            (self.ids, self.lens, x, small, *self.tables, *weights),
            [SMEM, SMEM] + [VMEM] * 4 + [HBM] * len(weights),
            (
                shape((t, 3 * d), BF),
                shape((self.heads, t, t), F32),
                shape((t, 2 * d), BF),
                shape((t, d), F32),
            ),
            (VMEM,) * 4,
            [self.part, pltpu.VMEM((t, t), F32), self.sem],
            2 * t * d * d * 4 + 4 * self.heads * t * t * LANES,
        )

    def feed_forward(self, layer, resid, small, weights):
        p = self.plan
        t, d = p.tok, p.width
        return call(
            functools.partial(feed_forward, p, layer),
            f"feed_forward_{layer}",
            (self.ids, resid, small, *weights),
            [SMEM, VMEM, VMEM] + [HBM] * len(weights),
            (
                shape((t, (PARTS + 1) * d), BF),
                shape((t, PARTS * d), F32),
                shape((t, d), BF),
            ),
            (VMEM,) * 3,
            [self.part, self.tall, self.sem, self.sem],
            2 * t * d * d * 8,
        )

    def weight_grad(self, layer, kind, body, args, specs, flops):
        p = self.plan
        if not p.direct:
            dims = (PARTS * p.width, BLOCK) if kind == "down" else (PARTS, p.width, BLOCK)
            outs = (shape(dims, BF),)
        else:
            halved = (p.groups, p.rows // 2) if p.rows_first(layer, kind) else (p.groups // 2, p.rows)
            piece = (p.tall * PARTS, BLOCK) if kind == "down" else (PARTS, p.tall, BLOCK)
            outs = (shape((*halved, *piece), BF),) * 2
        dims = (PARTS * p.width, BLOCK) if kind == "down" else (PARTS, p.width, BLOCK)
        return pl.pallas_call(
            body,
            out_shape=outs,
            grid_spec=pltpu.PrefetchScalarGridSpec(
                num_scalar_prefetch=1,
                grid=(1,),
                in_specs=specs,
                out_specs=(HBM,) * len(outs),
                scratch_shapes=[pltpu.VMEM(dims, BF), self.sem],
            ),
            name=f"{kind}_grad_{layer}",
            cost_estimate=pl.CostEstimate(flops=flops, transcendentals=0, bytes_accessed=1 << 22),
        )(self.ids, *args)

    def down_grad(self, layer, acts, d, at):
        p = self.plan
        left = pl.BlockSpec((p.tok, PARTS * p.width), lambda i, ids: (0, 0))
        right = pl.BlockSpec(d[0].shape, lambda i, ids: (0, 0))
        flops = 4 * p.tok * p.width * PARTS * BLOCK
        return self.weight_grad(
            layer, "down", functools.partial(down_grad, p, p.rows_first(layer, "down"), at), (*acts, *d), [left] * 2 + [right] * 2, flops
        )

    def up_grad(self, layer, acts, d):
        p = self.plan
        left = pl.BlockSpec((p.tok, p.width), lambda i, ids: (0, PARTS))
        right = pl.BlockSpec(d[0].shape, lambda i, ids: (0, 0))
        flops = 4 * p.tok * p.width * PARTS * BLOCK
        return self.weight_grad(
            layer, "up", functools.partial(up_grad, p, p.rows_first(layer, "up")), (*acts, *d), [left] * 2 + [right] * 2, flops
        )

    def attend_grad(self, layer, acts, d):
        p = self.plan
        left = pl.BlockSpec(acts[0].shape, lambda i, ids: (0, 0))
        right = pl.BlockSpec(d[0].shape, lambda i, ids: (0, 0))
        flops = 4 * p.tok * p.width * PARTS * BLOCK
        return self.weight_grad(
            layer, "attend", functools.partial(attend_grad, p, p.rows_first(layer, "attend")), (*acts, *d), [left] * 2 + [right] * 2, flops
        )

    def feed_backward(self, layer, d_out, resid, slope, small, weights):
        p = self.plan
        t, d = p.tok, p.width
        return call(
            functools.partial(feed_backward, p, layer),
            f"feed_backward_{layer}",
            (self.ids, d_out, resid, slope, small, *weights),
            [SMEM] + [VMEM] * 4 + [HBM] * len(weights),
            (*(shape((t, PARTS * BLOCK), BF),) * 2, shape((t, d), F32), shape((2, d), F32)),
            (VMEM,) * 4,
            [self.part, self.tall, self.sem, self.sem],
            2 * t * d * d * 8,
        )

    def attend_backward(self, layer, x, d_resid, qkv, probs, small, weights):
        p = self.plan
        t, d = p.tok, p.width
        return call(
            functools.partial(attend_backward, p, layer),
            f"attend_backward_{layer}",
            (self.ids, x, d_resid, qkv, probs, small, *self.tables, *weights),
            [SMEM] + [VMEM] * 7 + [HBM] * len(weights),
            (*(shape((t, (PARTS + 1) * BLOCK), BF),) * 2, shape((t, d), BF), shape((2, d), F32)),
            (VMEM,) * 4,
            [self.part, pltpu.VMEM((t, d), BF), pltpu.VMEM((t, 3 * d), BF), self.sem],
            2 * t * d * d * 4 + 10 * self.heads * t * t * LANES,
        )

    def pack(self, shards):
        p = self.plan
        dims = (3 * PARTS, p.tall, BLOCK)
        specs = []
        for i, w in enumerate(shards):
            tall = p.tall * PARTS if i == len(shards) - 1 else p.tall
            specs.append(pl.BlockSpec((1, tall, w.shape[2]), lambda i, ids: (0, ids[1], 0)))
        whole = pl.BlockSpec(dims, lambda i, ids: (0, 0, 0))
        return pl.pallas_call(
            functools.partial(pack, p),
            out_shape=(shape(dims, BF),) * 2,
            grid_spec=pltpu.PrefetchScalarGridSpec(
                num_scalar_prefetch=1, grid=(1,), in_specs=specs, out_specs=(whole, whole)
            ),
            name="pack",
        )(self.ids, *shards)

    def final(self, kind, sources):
        p = self.plan
        share, d = p.width // p.rows, p.width
        dims = {"attend": ((share, 3 * d), (share, d)), "up": ((share, PARTS * d),), "down": ((share * PARTS, d),)}
        outs = tuple(shape((1, *dim), F32) for dim in dims[kind])
        specs = []
        for x, at in sources:
            specs.append(pl.BlockSpec((p.groups, PARTS, p.tall, BLOCK), lambda i, ids, at=at: (0, at, 0, 0)))
        return pl.pallas_call(
            functools.partial(final_layout, p, kind),
            out_shape=outs,
            grid_spec=pltpu.PrefetchScalarGridSpec(
                num_scalar_prefetch=1,
                grid=(1,),
                in_specs=specs,
                out_specs=tuple(pl.BlockSpec(o.shape, lambda i, ids: (0, 0, 0)) for o in outs),
            ),
            name=f"final_{kind}",
        )(self.ids, *(x for x, _ in sources))


def swap_cores(x):
    return lax.ppermute(x, "section", [(0, 1), (1, 0)])


def stage_bits(groups):
    bits = [1 << i for i in range(groups.bit_length() - 1)]
    turn = len(bits) // 2
    return bits, bits[turn:] + bits[:turn]


def swap_groups(x, groups, stage):
    pairs = []
    for core, bits in enumerate(stage_bits(groups)):
        pairs += [(core * groups + g, core * groups + (g ^ bits[stage])) for g in range(groups)]
    return lax.ppermute(x, ("section", "group"), pairs)


def along(x, distance):
    rows = lax.axis_size("dp")
    return lax.ppermute(x, "dp", [(i, (i + distance) % rows) for i in range(rows)])


def gate(x, after):
    return lax.optimization_barrier((x, *after))[0] if after else x


def swap_rows(x, bit):
    rows = lax.axis_size("dp")
    return lax.ppermute(x, "dp", [(i, i ^ bit) for i in range(rows)])


KINDS = ("attend", "up", "down")


def piece_of(plan, group, kind, shards):
    tall = plan.tall

    def cut(w, inside):
        if inside:
            w = lax.dynamic_slice_in_dim(w[0], group * (tall * PARTS), tall * PARTS, 0)
            return w.reshape(PARTS, tall, 2, BLOCK).transpose(2, 0, 1, 3)
        w = lax.dynamic_slice_in_dim(w[0], group * tall, tall, 0)
        return w.reshape(tall, -1, 2, BLOCK).transpose(2, 1, 0, 3)

    return jnp.concatenate([cut(w, kind == "down") for w in shards], axis=1)


def whole_of(plan, core, group, row, kind, shard, half_mine, half_theirs):
    groups, rows, tall = plan.groups, plan.rows, plan.tall
    tables = jnp.array(masks_of(groups, True), jnp.int32)
    first = core == 0
    halves = []
    for h in range(2):
        got = jnp.where(core == h, half_mine, half_theirs)
        got = jnp.take(got, jnp.argsort(group ^ tables[h]), axis=0)
        own = []
        for w in shard:
            if kind == "down":
                w = w[0].reshape(groups, PARTS, tall, 2, BLOCK)[:, :, :, h]
            else:
                w = w[0].reshape(groups, tall, -1, 2, BLOCK)[:, :, :, h].transpose(0, 2, 1, 3)
            own.append(w)
        own = jnp.concatenate(own, axis=1)[:, None]
        got = jnp.concatenate([got, own], axis=1)
        held = jnp.stack([row_from(plan, row, k) for k in range(rows - 1)] + [row])
        got = jnp.take(got, jnp.argsort(held), axis=1)
        if kind == "down":
            halves.append(got.transpose(1, 0, 2, 3, 4).reshape(PARTS * plan.width, BLOCK))
        else:
            halves.append(got.transpose(2, 1, 0, 3, 4).reshape(PARTS, plan.width, BLOCK))
    return jnp.stack(halves)


def ordered_grads(plan, kind, core, group, row, x):
    groups, rows, tall = plan.groups, plan.rows, plan.tall
    tables = jnp.array(masks_of(groups, False), jnp.int32)
    if kind == "down":
        x = x.reshape(rows, groups, PARTS, tall, BLOCK).transpose(1, 0, 2, 3, 4)
    else:
        x = x.reshape(PARTS, rows, groups, tall, BLOCK).transpose(2, 1, 0, 3, 4)
    x = jnp.take(x, group ^ jnp.where(core == 0, tables[0], tables[1]), axis=0)
    x = jnp.take(x, jnp.stack([row_to(plan, row, k) for k in range(rows)]), axis=1)
    return x[: groups // 2], x[groups // 2 :]


def on_device(
    tokens,
    cotangent,
    lengths,
    attend_gain,
    attend_bias,
    qkv_weight,
    out_weight,
    feed_gain,
    feed_bias,
    up_weight,
    down_weight,
):
    core = lax.axis_index("section")
    group = lax.axis_index("group")
    row = lax.axis_index("dp")
    groups = lax.axis_size("group")
    rows = lax.axis_size("dp")
    stages = groups.bit_length() - 1
    tok, width = tokens.shape[1:]
    plan = Plan(groups, rows, tok, width)
    few = plan.few
    first = core == 0
    share = width // rows
    ids = jnp.stack([core, group, row]).astype(jnp.int32)
    lens = lax.dynamic_index_in_dim(lengths, core, 0, False)[0]

    shards = {"attend": (qkv_weight, out_weight), "up": (up_weight,), "down": (down_weight,)}
    chunks = [(layer, kind) for layer in range(2) for kind in KINDS]
    n_chunks = len(chunks)
    x0 = lax.dynamic_index_in_dim(tokens, core, 0, False)
    cot = lax.dynamic_index_in_dim(cotangent, core, 0, False)
    cosine, sine, _ = rope_tables(lens, tok)
    kernels = Kernels(plan, ids, lens, (cosine, sine), width // HEAD_DIM)
    history = {}
    pieces, bufs, gots, theirs, saved = {}, {}, {}, {}, {}
    xs = {0: x0}
    small = jnp.stack([attend_gain[0], attend_bias[0], feed_gain[0], feed_bias[0]])[None]

    if plan.direct:
        keep, send = kernels.pack([w for kind in KINDS for w in shards[kind]])
    else:
        both = jnp.concatenate([piece_of(plan, group, kind, shards[kind]) for kind in KINDS], axis=1)
        keep = lax.dynamic_index_in_dim(both, core, 0, False)
        send = lax.dynamic_index_in_dim(both, 1 - core, 0, False)
    got = swap_cores(send)
    for layer in range(2):
        part = jnp.where(core == layer, keep, got)
        for i, kind in enumerate(KINDS):
            pieces[layer, kind] = part[i * PARTS : (i + 1) * PARTS][None, None]

    def weights_of(layer, kind):
        parts = [*bufs[layer, kind], *gots[layer, kind]]
        if plan.direct:
            if kind == "down":
                parts = [p.reshape(*p.shape[:2], PARTS * plan.tall, BLOCK) for p in parts]
            return (*shards[kind], *theirs[kind], *parts)
        mine, other = (jnp.concatenate(p, axis=0) for p in (parts[:2], parts[2:]))
        shard = [jnp.where(core == layer, a, b) for a, b in zip(shards[kind], theirs[kind])]
        return (whole_of(plan, core, group, row, kind, shard, mine, other),)

    def run_attend(layer, after):
        x = gate(xs[layer], after)
        out = kernels.attend_forward(layer, x, smalls[layer], weights_of(layer, "attend"))
        saved[layer, "attend"] = out
        return out[3]

    def run_feed(layer, after):
        resid = gate(saved[layer, "attend"][3], after)
        weights = weights_of(layer, "up") + weights_of(layer, "down")
        *out, y = kernels.feed_forward(layer, resid, smalls[layer], weights)
        saved[layer, "feed"] = out
        xs[layer + 1] = y
        return y

    row_bits = [1 << i for i in range(rows.bit_length() - 1)]
    hops = len(row_bits) if few else 1
    depth = hops + stages
    kernel_at = {depth + SHIFT: (run_attend, 0), depth + 2 + SHIFT: (run_feed, 0), depth + 3 + SHIFT: (run_attend, 1)}
    small_steps = row_bits + [0]
    gotten, to_swap, acts_too = {}, {}, {}
    for slot in range(n_chunks + depth + 1):
        after = history.get(slot - DEPTH, [])
        done = []
        for stage in range(depth, -1, -1):
            c = slot - stage
            if not 0 <= c < n_chunks:
                continue
            chunk = chunks[c]
            if stage == depth:
                gots[chunk].append(swap_cores(gate(bufs[chunk][1], after)))
                done.append(gots[chunk][-1])
                continue
            if stage < hops:
                piece = pieces[chunk]
                if few:
                    got = swap_rows(gate(piece, after), row_bits[hops - 1 - stage])
                    pieces[chunk] = jnp.concatenate([piece, got], axis=1)
                    gotten.setdefault(chunk, []).append(got)
                else:
                    got = lax.all_gather(gate(piece[0, 0], after), "dp")
                    back = (row - 1 - jnp.arange(rows - 1)) % rows
                    gotten[chunk] = [jnp.take(got, back, axis=0)[None]]
                done.append(got)
                continue
            if stage == hops:
                bufs[chunk] = jnp.concatenate(gotten[chunk], axis=1)
            buf = bufs[chunk]
            got = swap_groups(gate(buf, after), groups, stage - hops)
            done.append(got)
            if stage + 1 < depth:
                bufs[chunk] = jnp.concatenate([buf, got], axis=0)
            else:
                bufs[chunk] = [buf, got]
                gots[chunk] = [swap_cores(gate(buf, after))]
                done.append(gots[chunk][0])
        if few and slot < len(small_steps):
            bit = small_steps[slot]
            held = gate(small, history.get(slot - 1, []))
            got = swap_rows(held, bit) if bit else swap_cores(held)
            done.append(got)
            small = jnp.concatenate([small, got])
        elif slot == 0:
            small = lax.all_gather(small, ("section", "dp"))
        if slot == (len(small_steps) if few else 1):
            got = small.reshape(2, rows, PARTS, share)
            if few:
                got = jnp.take(got, row ^ jnp.arange(rows), axis=1)
                got = jnp.take(got, core ^ jnp.arange(2), axis=0)
            smalls = got.transpose(0, 2, 1, 3).reshape(2, PARTS, width).astype(F32)
        if 1 <= slot <= len(KINDS):
            kind = KINDS[slot - 1]
            theirs[kind] = tuple(swap_cores(gate(w, history[slot - 1])) for w in shards[kind])
            done += theirs[kind]
        for (layer, kind), acts in list(to_swap.items()):
            acts_too[layer, kind] = swap_cores(gate(acts, after))
            done.append(acts_too[layer, kind])
            del to_swap[layer, kind]
        if slot in kernel_at:
            run, layer = kernel_at[slot]
            done.append(run(layer, history[slot - 1]))
            if run is run_attend:
                to_swap[layer, "attend"] = saved[layer, "attend"][2]
            else:
                to_swap[layer, "feed"] = saved[layer, "feed"][0]
        history[slot] = done
    run_feed(1, [])
    to_swap[1, "feed"] = saved[1, "feed"][0]
    for (layer, kind), acts in to_swap.items():
        acts_too[layer, kind] = swap_cores(acts)

    backs, sums, d_cols = [None, None], {}, {}
    order = [(layer, kind) for layer in (1, 0) for kind in ("down", "up", "attend")]
    halves = lax.dynamic_slice_in_dim(cotangent, core * BLOCK, BLOCK, 2)
    d_cols[2, "attend"] = (
        lax.dynamic_index_in_dim(halves, core, 0, False),
        lax.dynamic_index_in_dim(halves, 1 - core, 0, False),
    )
    d_outs = {1: cot}
    d_resids = {}

    def chain_feed(layer, after):
        weights = weights_of(layer, "up") + weights_of(layer, "down")
        resid, slope = saved[layer, "attend"][3], saved[layer, "feed"][1]
        own, send, d_resids[layer], sums[layer, "up"] = kernels.feed_backward(
            layer, gate(d_outs[layer], after), resid, slope, smalls[layer], weights
        )
        d_cols[layer, "up"] = (own, swap_cores(send))
        return send

    def chain_attend(layer, after):
        qkv, probs = saved[layer, "attend"][:2]
        own, send, dx, sums[layer, "attend"] = kernels.attend_backward(
            layer,
            xs[layer],
            gate(d_resids[layer], after),
            qkv,
            probs,
            smalls[layer],
            weights_of(layer, "attend"),
        )
        d_cols[layer, "attend"] = (own, swap_cores(send))
        backs[layer] = d_outs[layer - 1] = dx
        return send

    def weight_grad(layer, kind, after):
        if kind == "attend":
            acts = (saved[layer, "attend"][2], acts_too[layer, "attend"])
            own, other = d_cols[layer, "attend"]
            outs = kernels.attend_grad(layer, acts, (gate(own, after), other))
        else:
            acts = (saved[layer, "feed"][0], acts_too[layer, "feed"])
            own, other = d_cols[layer, "up"] if kind == "up" else d_cols[layer + 1, "attend"]
            d = (gate(own, after), other)
            if kind == "up":
                outs = kernels.up_grad(layer, acts, d)
            else:
                outs = kernels.down_grad(layer, acts, d, 0 if layer == 1 else PARTS * BLOCK)
        if not plan.direct:
            return ordered_grads(plan, kind, core, group, row, outs[0])
        return [x.reshape(*x.shape[:2], PARTS, plan.tall, BLOCK) for x in outs]

    def total_of(parts):
        total = parts[0].astype(F32)
        for part in parts[1:]:
            total = total + part.astype(F32)
        return total.astype(BF)

    def way_of(layer, kind):
        over_groups = [(0, i) for i in range(stages)]
        over_rows = [(1, bit) for bit in row_bits] if few else [(1, 0)]
        return over_rows + over_groups if plan.rows_first(layer, kind) else over_groups + over_rows

    last = stages + hops

    def step(layer, kind, parts, stage, after):
        if stage == 0:
            send = gate(parts["send"], after)
            axis, bit = way_of(layer, kind)[0]
            got = swap_rows(send, bit) if axis else swap_groups(send, groups, bit)
            parts["sum"] = [parts["keep"], got]
            parts["left"] = list(parts["keep"].shape[:2])
            return got
        axis, bit = way_of(layer, kind)[stage]
        if axis == 1 and not few:
            send = total_of([p[0] for p in parts["sum"]])
            held = jnp.argsort(jnp.stack([row_to(plan, row, k) for k in range(rows)]))
            send = gate(jnp.take(send, held, axis=0), after)
            got = lax.psum_scatter(send, "dp", scatter_dimension=0, tiled=True)
            parts["sum"] = [got[None]]
            parts["left"] = [1, 1]
            return got
        low, high = [0, 0], list(parts["left"])
        low[axis] = high[axis] // 2
        send = total_of([p[low[0] : high[0], low[1] : high[1]] for p in parts["sum"]])
        parts["left"][axis] //= 2
        send = gate(send, after)
        sends.append(send)
        got = swap_groups(send, groups, bit) if axis == 0 else swap_rows(send, bit)
        parts["sum"] = parts["sum"] + [got]
        return got

    def result_of(parts):
        return total_of([p[:1, 0] for p in parts["sum"]])

    def home(low, high):
        got = swap_cores(jnp.where(first, high, low))
        keep = jnp.where(first, low, high)
        return jnp.where(first, jnp.stack([keep, got]), jnp.stack([got, keep]))

    layer_out = home(xs[1], xs[2])
    history, sends = {}, []
    chain_feed(1, [])
    keep, send = weight_grad(*order[0], [])
    live = {0: {"keep": keep, "send": send}}
    def outside(x):
        return x.transpose(0, 3, 2, 1, 4).reshape(1, share, -1).astype(F32)

    def result_for(kind):
        sources = []
        for source_layer in range(2):
            for name, (layer, kinds) in gathers.items():
                if layer == source_layer and kind in kinds:
                    sources += [(x, kinds.index(kind)) for x in final[name]]
        if plan.direct:
            return kernels.final(kind, sources)
        parts = [x[:, i * PARTS : (i + 1) * PARTS] for x, i in sources]
        tables = jnp.array(masks_of(groups, False), jnp.int32)
        low = jnp.take(jnp.where(first, parts[0], parts[3]), jnp.argsort(group ^ tables[0]), axis=0)
        high = jnp.take(jnp.where(first, parts[1], parts[2]), jnp.argsort(group ^ tables[1]), axis=0)
        x = jnp.stack([low, high], axis=1)
        if kind == "attend":
            return (outside(x[:, :, 0:3]), outside(x[:, :, 3:4]))
        if kind == "up":
            return (outside(x),)
        return (x.transpose(0, 2, 3, 1, 4).reshape(1, -1, width).astype(F32),)

    final, results = {}, {}
    gathers = GATHERS
    small_sum, small_stage, smalls_seen = None, 0, []
    beside = [[(chain_attend, 1)], [(chain_feed, 0)], [(chain_attend, 0)], [], []]
    for slot in range(n_chunks + last + stages + 1):
        after = history.get(slot - DEPTH_BACK, [])
        done = []
        sends.clear()
        for c in range(n_chunks):
            if 0 <= slot - c < last:
                held = smalls_seen[-LATE : len(smalls_seen) - LATE + 1] if LATE and c == n_chunks - 1 else []
                done.append(step(*order[c], live[c], slot - c, after + held))
        for name, (layer, kinds) in gathers.items():
            stage = slot - last - max(order.index((layer, kind)) for kind in kinds)
            if stage == 0:
                final[name] = jnp.concatenate([result_of(live[order.index((layer, k))]) for k in kinds], axis=1)
            if 0 <= stage < stages:
                got = swap_groups(final[name], groups, stages - 1 - stage)
                final[name] = jnp.concatenate([final[name], got], axis=0)
            elif stage == stages:
                held = final[name]
                if name == "attend":
                    held = gate(held, [layer_out, input_grad, *results[EARLY]] if EARLY else [layer_out, input_grad])
                got = lax.ppermute(held, "section", [(1 - layer, layer)])
                final[name] = (final[name], got)
                if name == "feed":
                    for kind in ("down", "up"):
                        results[kind] = result_for(kind)
        if slot + 1 < n_chunks:
            before = history.get(slot - 1, []) if OLD else list(sends)
            now = done[-BESIDE:] if BESIDE else []
            extra = []
            for run, layer in beside[slot]:
                if order[slot + 1][1] == "down":
                    continue
                extra.append(run(layer, before))
            keep, send = weight_grad(*order[slot + 1], extra or before)
            live[slot + 1] = {"keep": keep, "send": gate(send, now)}
            if order[slot + 1][1] == "down":
                for run, layer in beside[slot]:
                    extra.append(run(layer, [send]))
            if OLD:
                done.append(send)
        if slot + 1 == n_chunks:
            input_grad = home(*backs)
            small_sum = jnp.stack([jnp.concatenate([sums[i, "attend"], sums[i, "up"]]) for i in range(2)])
        if small_sum is not None and small_stage <= stages + len(row_bits):
            held = gate(small_sum, history.get(slot - 1, []))
            if small_stage == 0:
                got = swap_cores(held)
            elif small_stage <= stages:
                got = swap_groups(held, groups, small_stage - 1)
            else:
                got = swap_rows(held, row_bits[small_stage - stages - 1])
            small_stage += 1
            small_sum = small_sum + got
            smalls_seen.append(small_sum)
        history[slot] = done

    qkv_grad, out_grad = result_for("attend")
    (up_grad,) = results["up"]
    (down_grads,) = results["down"]

    small_grads = small_sum
    own = lax.dynamic_index_in_dim(small_grads, core, 0, False)
    own = lax.dynamic_slice_in_dim(own, row * share, share, 1)
    return (
        layer_out[None],
        input_grad[None],
        own[0][None],
        own[1][None],
        qkv_grad,
        out_grad,
        own[2][None],
        own[3][None],
        up_grad,
        down_grads,
    )


def solution(mesh):
    placed = (
        P(None, ("group", "dp"), None),
        P(None, ("group", "dp"), None),
        P(None, ("group", "dp"), None),
        P("section", "dp"),
        P("section", "dp"),
        P("section", "dp", None),
        P("section", "dp", None),
        P("section", "dp"),
        P("section", "dp"),
        P("section", "dp", None),
        P("section", "dp", None),
    )
    return jax.shard_map(
        on_device,
        mesh=mesh,
        in_specs=placed,
        out_specs=(
            P("section", None, ("group", "dp"), None),
            P("section", None, ("group", "dp"), None),
            P("section", "dp"),
            P("section", "dp"),
            P("section", "dp", None),
            P("section", "dp", None),
            P("section", "dp"),
            P("section", "dp"),
            P("section", "dp", None),
            P("section", "dp", None),
        ),
        check_vma=False,
    )
```
